128 devices in a mesh: row: 8 (over x_hi, z), col: 8 (over x_lo, y), layer: 2 (over core).
Axes of the slice: x: 4 (x_hi: 2, x_lo: 2; x = x_hi * 2 + x_lo), y: 4, z: 4, core: 2. Of those that a mesh axis runs over, the one named last changes fastest.
Arguments:
- matrix: float32 [32, 512, 32, 512], P('row', None, 'col', 'layer'), may hold values from -40 to 40, as said below
- transforms: float32 [1, 16, 1024, 1024], P(None, 'row', ('col', 'layer')), may hold values from -0.1875 to 0.1875
Outputs:
- swept: float32 [32, 512, 32, 512], P('row', None, 'col', 'layer')
The draws below stay inside these ranges and needn't reach their ends.
Inputs may be any that keep to these rules, and one draw needn't show every extreme that they name: `matrix`: symmetric: entry [i, a, j, b] equals entry [j, b, i, a].
All inputs are finite; a program needn't handle non-finite values.
Results may differ from the reference program's by a relative error of at most 0.0001.
Values sent between devices are 32-bit elements; how exact they have to be, the bound alone decides.
No kernel may reach another device: no remote copies, remote signals or barrier semaphores. Data moves between devices by JAX's collectives and lax.ppermute only.
A program may use at most 192 MiB of HBM per device.

```python
import jax
import jax.numpy as jnp
from jax import lax

BS = 512
STEPS = 1
PAIRS = 16
NBLK = 32


def draw_matrix(key, part):
    gaussian = jax.random.normal(key, (NBLK * BS, NBLK * BS), jnp.float32)
    symmetric = (gaussian + gaussian.T) * 0.7071067811865476
    return symmetric.reshape(NBLK, BS, NBLK, BS)


def steps_of(own_key, dims, pieces, low, largest):
    def one(position, parts):
        heights = jax.random.uniform(jax.random.fold_in(jax.random.fold_in(own_key, 6), position), (parts,), jnp.float32, low / len(pieces), largest / len(pieces))
        return jnp.repeat(jnp.exp(heights), dims[position] // parts).reshape((-1,) + (1,) * (len(dims) - position - 1))

    factor_of = one(*pieces[0])
    for cut in pieces[1:]:
        factor_of = factor_of * one(*cut)
    return factor_of


def centred(own_key, dims, spread, limit, pieces=(), held_as=jnp.bfloat16):
    loudness = steps_of(own_key, dims, pieces, -0.22, 0.18) if pieces else 1.0
    result = jax.random.normal(own_key, dims, jnp.float32) * spread * loudness
    return jnp.minimum(jnp.maximum(result, -limit), limit).astype(held_as)


def setup_inputs(seed: int = 0) -> dict:
    keys = jax.random.split(jax.random.key(seed), 3)
    matrix = draw_matrix(jax.random.fold_in(keys[2], 71), 0)
    transforms = centred(keys[1], (STEPS, PAIRS, 2 * BS, 2 * BS), (2 * BS) ** -0.5, 0.1875, ((1, 8), (2, 16)), jnp.float32)
    return dict(matrix=matrix, transforms=transforms)


def sweep_order(count):
    slot_ids = jnp.arange(count, dtype=jnp.int32)
    is_odd = slot_ids % 2
    source = jnp.where(is_odd == 0, slot_ids - 2, slot_ids + 2)
    source = jnp.where(slot_ids == 0, 0, source)
    source = jnp.where(slot_ids == 2, 1, source)
    source = jnp.where(slot_ids == count - 1, count - 2, source)
    return source.astype(jnp.int32)


def reference(matrix, transforms):
    source = sweep_order(NBLK)
    current = matrix
    for step_index in range(STEPS):
        blocks = transforms[step_index]
        grouped = current.reshape(PAIRS, 2 * BS, PAIRS, 2 * BS)
        left_part = jnp.einsum("pkqb,pka->paqb", grouped, blocks, precision=lax.Precision.HIGHEST)
        rotated_pairs = jnp.einsum("paqk,qkb->paqb", left_part, blocks, precision=lax.Precision.HIGHEST)
        rotated = rotated_pairs.reshape(NBLK, BS, NBLK, BS)
        current = jnp.take(jnp.take(rotated, source, axis=0), source, axis=2)
    return current
```

```python
import jax
import jax.numpy as jnp
from jax import lax
from jax.experimental import pallas as pl
from jax.experimental.pallas import tpu as pltpu
from jax.sharding import PartitionSpec as P

F32 = jnp.float32
BF16 = jnp.bfloat16
AXES = ("row", "col", "layer")
VMEM_LIMIT = 56 * 1024 * 1024


def route(place):
    pairs = []
    for r in range(8):
        for c in range(8):
            for l in range(2):
                to = place(r, c, l)
                if to is not None:
                    pairs.append(((r * 8 + c) * 2 + l, (to[0] * 8 + to[1]) * 2 + to[2]))
    return pairs


def send(x, place):
    return lax.ppermute(x, AXES, route(place))


def split(x):
    high = x.astype(BF16)
    return high, (x - high.astype(F32)).astype(BF16)


def product(ah, al, bh, bl):
    def dot(a, b):
        return jnp.dot(a, b, preferred_element_type=F32)

    return dot(ah, bh) + (dot(ah, bl) + dot(al, bh))


def left_kernel(j_ref, own_ref, other_ref, *refs):
    yh_ref, yl_ref, jh, jl = refs[-4:]

    @pl.when(pl.program_id(0) == 0)
    def _():
        for k in range(4):
            cols = pl.ds(k * 256, 256)
            high, low = split(j_ref[cols, :].T)
            jh[:, cols] = high
            jl[:, cols] = low

    mh, ml = split(jnp.concatenate([own_ref[0], other_ref[0]], axis=1))
    for a in range(4):
        rows = pl.ds(a * 256, 256)
        high, low = split(product(jh[rows, :], jl[rows, :], mh, ml))
        yh_ref[rows, :] = high
        yl_ref[rows, :] = low


def left_product(pair, panel, own, other, previous):
    block = pl.BlockSpec((1, 1024, 256), lambda s: (s, pair, 0))
    out = pl.BlockSpec((1024, 512), lambda s: (pair, s))
    shape = jax.ShapeDtypeStruct((2048, 2048), BF16)
    extra = [] if previous is None else list(previous)
    return pl.pallas_call(
        left_kernel,
        grid=(4,),
        in_specs=[pl.BlockSpec((1024, 1024), lambda s: (0, 0)), block, block]
        + [pl.BlockSpec(memory_space=pl.ANY)] * len(extra),
        out_specs=[out, out],
        out_shape=[shape, shape],
        scratch_shapes=[pltpu.VMEM((1024, 1024), BF16), pltpu.VMEM((1024, 1024), BF16)],
        input_output_aliases={3: 0, 4: 1} if extra else {},
        compiler_params=pltpu.CompilerParams(vmem_limit_bytes=VMEM_LIMIT),
        cost_estimate=pl.CostEstimate(
            flops=3 * 2 * 1024 * 1024 * 2048, bytes_accessed=20 << 20, transcendentals=0
        ),
        name="left_product",
    )(panel, own, other, *extra)


def holders(r):
    up = (r & 4) | ((r + 3) & 3)
    down = (r & 4) | ((r + 1) & 3)
    far = (r & 4) | ((r + 2) & 3)
    return [r, r ^ 4, up, up ^ 4, down, down ^ 4, far, far ^ 4]


def right_kernel(where, yh_ref, yl_ref, *refs):
    pieces = refs[:8]
    up_ref, down_ref, first_ref, jh, jl = refs[8], refs[9], refs[10], refs[-2], refs[-1]
    stay_refs = refs[11:-2]
    q = pl.program_id(0)
    slot = pl.program_id(1)
    row_pos = where[0]
    layer = where[2]

    @pl.when((q == 0) & (slot == 0))
    def _():
        for start, piece in zip(holders(row_pos), pieces):
            base = (start ^ (2 * layer)) * 128
            for pair in range(2):
                for half in range(2):
                    high, low = split(piece[0, pair, half])
                    rows = pl.ds(pl.multiple_of(base + half * 64, 64), 64)
                    jh[pair, rows, :] = high
                    jl[pair, rows, :] = low

    block = product(yh_ref[...], yl_ref[...], jh[q], jl[q])

    def keep(index, value):
        if len(stay_refs) == 1:
            stay_refs[0][index, q] = value
        else:
            for pair in range(2):

                @pl.when(q == pair)
                def _(pair=pair):
                    stay_refs[pair][index] = value

    @pl.when(slot == 0)
    def _():
        first_ref[q] = block

        @pl.when(row_pos > 0)
        def _():
            keep(1, block)

    @pl.when(slot == 1)
    def _():
        down_ref[q] = block

        @pl.when(row_pos == 0)
        def _():
            keep(1, block)

    @pl.when(slot == 2)
    def _():
        up_ref[q] = block

    @pl.when(slot == 3)
    def _():
        keep(0, block)


def right_product(which, where, yh, yl, pieces, separate):
    y_block = pl.BlockSpec((512, 1024), lambda q, s, w: (s, q))
    piece = pl.BlockSpec((1, 2, 2, 64, 256), lambda q, s, w: (which, 0, 0, 0, 0))
    pair_block = pl.BlockSpec((2, 512, 256), lambda q, s, w: (0, 0, 0))
    pair_shape = jax.ShapeDtypeStruct((2, 512, 256), F32)
    if separate:
        stay_specs, stay_shapes = [pair_block] * 2, [pair_shape] * 2
    else:
        stay_specs = [pl.BlockSpec((2, 2, 512, 256), lambda q, s, w: (0, 0, 0, 0))]
        stay_shapes = [jax.ShapeDtypeStruct((2, 2, 512, 256), F32)]
    return pl.pallas_call(
        right_kernel,
        grid_spec=pltpu.PrefetchScalarGridSpec(
            num_scalar_prefetch=1,
            grid=(2, 4),
            in_specs=[y_block, y_block] + [piece] * 8,
            out_specs=[pair_block] * 3 + stay_specs,
            scratch_shapes=[pltpu.VMEM((2, 1024, 256), BF16)] * 2,
        ),
        out_shape=[pair_shape] * 3 + stay_shapes,
        compiler_params=pltpu.CompilerParams(vmem_limit_bytes=VMEM_LIMIT),
        cost_estimate=pl.CostEstimate(
            flops=3 * 2 * 2048 * 1024 * 512, bytes_accessed=24 << 20, transcendentals=0
        ),
        name="right_product",
    )(where, yh, yl, *pieces)


def fill_kernel(out_rows, choose, count, where, *refs):
    sources = refs[:count]
    out_ref, held, packed, in_sem, out_sem = refs[-5:]
    chosen = choose(where, sources)
    for k in range(2):
        for j in range(4):
            for condition, source in chosen[k][j]:

                @pl.when(condition)
                def _(source=source, k=k, j=j):
                    pltpu.make_async_copy(source, held.at[k, j], in_sem.at[k, j]).start()

    leaving = []
    for k in range(2):
        for j in range(4):
            pltpu.make_async_copy(chosen[k][j][0][1], held.at[k, j], in_sem.at[k, j]).wait()
            packed[k, :, j, :] = held[k, j]
        copy = pltpu.make_async_copy(packed.at[k], out_ref.at[out_rows[k]], out_sem.at[k])
        copy.start()
        leaving.append(copy)
    for copy in leaving:
        copy.wait()


def fill_rows(out_rows, choose, where, sources, previous):
    extra = [] if previous is None else [previous]
    count = len(sources)
    anywhere = pl.BlockSpec(memory_space=pl.ANY)

    def kernel(where, *refs):
        fill_kernel(out_rows, choose, count, where, *refs)

    return pl.pallas_call(
        kernel,
        grid_spec=pltpu.PrefetchScalarGridSpec(
            num_scalar_prefetch=1,
            grid=(1,),
            in_specs=[anywhere] * (count + len(extra)),
            out_specs=anywhere,
            scratch_shapes=[
                pltpu.VMEM((2, 4, 512, 256), F32),
                pltpu.VMEM((2, 512, 4, 256), F32),
                pltpu.SemaphoreType.DMA((2, 4)),
                pltpu.SemaphoreType.DMA((2,)),
            ],
        ),
        out_shape=jax.ShapeDtypeStruct((4, 512, 4, 256), F32),
        input_output_aliases={1 + count: 0} if extra else {},
        compiler_params=pltpu.CompilerParams(vmem_limit_bytes=VMEM_LIMIT),
        cost_estimate=pl.CostEstimate(flops=0, bytes_accessed=8 << 20, transcendentals=0),
        name="fill_rows",
    )(where, *sources, *extra)


def ring(piece):
    def across(r, c, l):
        return r ^ 4, c, l

    def above(r, c, l):
        return (r & 4) | ((r + 1) & 3), c, l

    def below(r, c, l):
        return (r & 4) | ((r + 3) & 3), c, l

    up = send(piece, above)
    down = send(piece, below)
    pair = send(piece, across)
    pair_up = send(pair, above)
    pair_down = send(pair, below)
    far = send(up, above)
    pair_far = send(pair_down, below)
    return [piece, pair, up, pair_up, down, pair_down, far, pair_far]


def step_up(axis):
    def place(r, c, l):
        to = [r, c, l]
        to[axis] += 1
        return to if to[axis] < 8 else None

    return place


def step_down(axis):
    def place(r, c, l):
        to = [r, c, l]
        to[axis] -= 1
        return to if to[axis] >= 0 else None

    return place


def shards(matrix, transforms):
    row_pos = lax.axis_index("row")
    col_pos = lax.axis_index("col")
    layer_pos = lax.axis_index("layer")
    where = jnp.stack([row_pos, col_pos, layer_pos]).astype(jnp.int32)
    mine = transforms[0]

    parts = mine.reshape(2, 64, 2, 2, 256)
    kept = lax.dynamic_index_in_dim(parts, layer_pos, 3, keepdims=False)
    crossing = lax.dynamic_index_in_dim(parts, 1 - layer_pos, 3, keepdims=False)

    def by_use(x):
        return jnp.stack([jnp.stack([x[0, :, 1], x[1, :, 0]]), jnp.stack([x[0, :, 0], x[1, :, 1]])])

    from_same = send(by_use(kept), lambda r, c, l: (c, r, l))
    from_cross = send(by_use(crossing), lambda r, c, l: (c, r, 1 - l))
    even = jnp.where(layer_pos == 0, from_same, from_cross)
    odd = jnp.where(layer_pos == 0, from_cross, from_same)
    piece = jnp.stack([even, odd], axis=2)
    pieces = ring(piece)

    panels = [lax.all_gather(mine[p], ("col", "layer"), axis=0, tiled=True) for p in range(2)]

    own = matrix.transpose(2, 0, 1, 3).reshape(4, 2048, 256)
    other = lax.ppermute(own, "layer", [(0, 1), (1, 0)])

    halves = left_product(0, panels[0], own, other, None)
    yh, yl = left_product(1, panels[1], own, other, halves)

    up, down, first, stay_down, stay_up = right_product(0, where, yh, yl, pieces, True)
    got_up = send(up, step_up(0))
    got_down = send(down, step_down(0))
    stay_got_up = send(stay_up, step_up(1))
    stay_got_down = send(stay_down, step_down(1))

    s_up, s_down, s_first, s_stay = right_product(1, where, yh, yl, pieces, False)
    s_got_up = send(s_up, step_up(0))
    s_got_down = send(s_down, step_down(0))

    top = jnp.where(row_pos == 0, first, got_up)
    bottom = jnp.where(row_pos == 7, up, got_down)
    moved_down = jnp.stack([top[0], bottom[0]])
    moved_up = jnp.stack([top[1], bottom[1]])
    moved_got_up = send(moved_up, step_up(1))
    moved_got_down = send(moved_down, step_down(1))

    def choose_stay(w, refs):
        stay, went_up, went_down, came_up, came_down = refs
        c = w[1]
        return [
            [
                [(c > 0, came_up.at[k]), (c == 0, stay.at[k, 0])],
                [(c >= 0, stay.at[k, 1])],
                [(c > 0, stay.at[k, 0]), (c == 0, went_down.at[k])],
                [(c < 7, came_down.at[k]), (c == 7, went_up.at[k])],
            ]
            for k in range(2)
        ]

    out = fill_rows(
        (1, 2), choose_stay, where, [s_stay, stay_up, stay_down, stay_got_up, stay_got_down], None
    )

    def choose_moved(w, refs):
        first_row, up_row, from_up, from_down, went_up, went_down, came_up, came_down = refs
        r, c = w[0], w[1]

        def stays(k, q, condition):
            if k == 0:
                return [
                    (condition & (r > 0), from_up.at[q]),
                    (condition & (r == 0), first_row.at[q]),
                ]
            return [
                (condition & (r < 7), from_down.at[q]),
                (condition & (r == 7), up_row.at[q]),
            ]

        return [
            [
                [(c > 0, came_up.at[k])] + stays(k, 0, c == 0),
                stays(k, 1, c >= 0),
                [(c == 0, went_down.at[k])] + stays(k, 0, c > 0),
                [(c < 7, came_down.at[k]), (c == 7, went_up.at[k])],
            ]
            for k in range(2)
        ]

    return fill_rows(
        (0, 3),
        choose_moved,
        where,
        [s_first, s_up, s_got_up, s_got_down, moved_up, moved_down, moved_got_up, moved_got_down],
        out,
    )


def solution(mesh):
    return jax.shard_map(
        shards,
        mesh=mesh,
        in_specs=(P("row", None, "col", "layer"), P(None, "row", ("col", "layer"), None)),
        out_specs=P("row", None, "col", "layer"),
        check_vma=False,
    )
```

```python
import jax
import jax.numpy as jnp
from jax import lax
from jax.experimental import pallas as pl
from jax.experimental.pallas import tpu as pltpu
from jax.sharding import PartitionSpec as P

F32 = jnp.float32
BF16 = jnp.bfloat16
AXES = ("row", "col", "layer")
VMEM_LIMIT = 58 * 1024 * 1024
EARLY = (0, 1, 2, 4)
LATE = (3, 5, 6, 7)
ANYWHERE = pl.BlockSpec(memory_space=pl.ANY)


def route(place):
    pairs = []
    for r in range(8):
        for c in range(8):
            for l in range(2):
                to = place(r, c, l)
                if to is not None:
                    pairs.append(((r * 8 + c) * 2 + l, (to[0] * 8 + to[1]) * 2 + to[2]))
    return pairs


def send(x, place):
    return lax.ppermute(x, AXES, route(place))


def in_chip(x):
    return lax.ppermute(x, "layer", [(0, 1), (1, 0)])


def split(x):
    high = x.astype(BF16)
    return high, (x - high.astype(F32)).astype(BF16)


def product(ah, al, bh, bl):
    def dot(a, b):
        return jnp.dot(a, b, preferred_element_type=F32)

    return dot(ah, bh) + (dot(ah, bl) + dot(al, bh))


def holders(i):
    up = (i & 4) | ((i + 3) & 3)
    down = (i & 4) | ((i + 1) & 3)
    far = (i & 4) | ((i + 2) & 3)
    return [i, i ^ 4, up, up ^ 4, down, down ^ 4, far, far ^ 4]


def turned(ref, index, pair, cols):
    rows = jnp.concatenate([ref[index, 0, pair, :, cols], ref[index, 1, pair, :, cols]], axis=0)
    return split(rows.T)


def halves_of_matrix(own_refs, other_refs, mh, ml):
    for n in range(4):
        for m in range(2):
            for k, block in enumerate((own_refs[n][m], other_refs[2 * n + m][...])):
                high, low = split(block)
                lanes = slice(m * 512 + k * 256, m * 512 + k * 256 + 256)
                mh[n * 128 : n * 128 + 128, lanes] = high
                ml[n * 128 : n * 128 + 128, lanes] = low


def early_kernel(where, *refs):
    ours, theirs = refs[:4], refs[4:8]
    own_refs, other_refs = refs[8:12], refs[12:20]
    y_ref, held, jh, jl, mh, ml, sem = refs[20:]
    pair = pl.program_id(0)
    layer = where[2]

    @pl.when(pair == 0)
    def _():
        for i in range(4):

            @pl.when(layer == 0)
            def _(i=i):
                pltpu.make_async_copy(ours[i], held.at[i], sem.at[i]).start()

            @pl.when(layer == 1)
            def _(i=i):
                pltpu.make_async_copy(theirs[i], held.at[i], sem.at[i]).start()

    halves_of_matrix(own_refs, other_refs, mh, ml)

    @pl.when(pair == 0)
    def _():
        for i in range(4):
            pltpu.make_async_copy(ours[i], held.at[i], sem.at[i]).wait()

    for i in range(4):
        for half in range(4):
            high, low = turned(held, i, pair, pl.ds(half * 256, 256))
            jh[half * 256 : half * 256 + 256, i * 128 : i * 128 + 128] = high
            jl[half * 256 : half * 256 + 256, i * 128 : i * 128 + 128] = low
    for a in range(4):
        rows = pl.ds(a * 256, 256)
        y_ref[rows, :] = product(jh[rows, :], jl[rows, :], mh[...], ml[...])


def matrix_pieces(which, pair_of):
    def rows(i):
        return lambda step, w: pair_of(step, w) * 8 + holders(w[1])[i]

    own = [pl.BlockSpec((2, 128, 256), lambda s, w, f=rows(i): (w[2], f(s, w), 0)) for i in which]
    other = [pl.BlockSpec((128, 256), lambda s, w, f=rows(i): (f(s, w), 0)) for i in which]
    return own + [spec for spec in other for m in range(2)]


def early_product(where, pieces, crossed, own, other):
    return pl.pallas_call(
        early_kernel,
        grid_spec=pltpu.PrefetchScalarGridSpec(
            num_scalar_prefetch=1,
            grid=(2,),
            in_specs=[ANYWHERE] * 8 + matrix_pieces(EARLY, lambda p, w: p),
            out_specs=pl.BlockSpec((1024, 1024), lambda p, w: (p, 0)),
            scratch_shapes=[
                pltpu.VMEM((4, 2, 2, 64, 1024), F32),
                pltpu.VMEM((1024, 512), BF16),
                pltpu.VMEM((1024, 512), BF16),
                pltpu.VMEM((512, 1024), BF16),
                pltpu.VMEM((512, 1024), BF16),
                pltpu.SemaphoreType.DMA((4,)),
            ],
        ),
        out_shape=jax.ShapeDtypeStruct((2048, 1024), F32),
        compiler_params=pltpu.CompilerParams(vmem_limit_bytes=VMEM_LIMIT),
        cost_estimate=pl.CostEstimate(
            flops=3 * 2 * 2048 * 512 * 1024, bytes_accessed=24 << 20, transcendentals=0
        ),
        name="early_product",
    )(
        where,
        *[pieces[i] for i in EARLY],
        *[crossed[i] for i in EARLY],
        *[own] * 4,
        *[other[m] for n in range(4) for m in range(2)],
    )


def slot_of(moving, step, row_pos):
    edge = (row_pos == 0).astype(jnp.int32)
    if moving:
        return jnp.where(step == 0, 1 - edge, 2)
    return jnp.where(step == 0, 3, edge)


def late_kernel(moving, where, *refs):
    ours, theirs = refs[:8], refs[8:16]
    y_ref = refs[16]
    own_refs, other_refs = refs[17:21], refs[21:29]
    outs = refs[29:-14]
    held_a, held_b, jh, jl, mh, ml, yh, yl, qh, ql, done, sem_a, sem_b, sem_out = refs[-14:]
    step = pl.program_id(0)
    row_pos, layer = where[0], where[2]
    slot = slot_of(moving, step, row_pos)
    pair = slot // 2

    @pl.when(step == 0)
    def _():
        for n, i in enumerate(LATE):

            @pl.when(layer == 0)
            def _(n=n, i=i):
                pltpu.make_async_copy(ours[i], held_a.at[n], sem_a.at[n]).start()

            @pl.when(layer == 1)
            def _(n=n, i=i):
                pltpu.make_async_copy(theirs[i], held_a.at[n], sem_a.at[n]).start()

        for i in range(8):

            @pl.when(layer == 0)
            def _(i=i):
                pltpu.make_async_copy(theirs[i].at[:, 0], held_b.at[i], sem_b.at[i]).start()

            @pl.when(layer == 1)
            def _(i=i):
                pltpu.make_async_copy(ours[i].at[:, 1], held_b.at[i], sem_b.at[i]).start()

    halves_of_matrix(own_refs, other_refs, mh, ml)

    @pl.when(step == 0)
    def _():
        for n, i in enumerate(LATE):
            pltpu.make_async_copy(ours[i], held_a.at[n], sem_a.at[n]).wait()

    for n in range(4):
        for a in range(2):
            cols = pl.ds(pl.multiple_of((slot % 2) * 512 + a * 256, 256), 256)
            high, low = turned(held_a, n, pair, cols)
            jh[a * 256 : a * 256 + 256, n * 128 : n * 128 + 128] = high
            jl[a * 256 : a * 256 + 256, n * 128 : n * 128 + 128] = low

    for h in range(2):
        cols = slice(h * 512, h * 512 + 512)
        high, low = split(y_ref[:, cols] + product(jh[...], jl[...], mh[:, cols], ml[:, cols]))
        yh[:, cols] = high
        yl[:, cols] = low

    @pl.when(step == 0)
    def _():
        for i, start in enumerate(holders(row_pos)):
            pltpu.make_async_copy(ours[i].at[:, 0], held_b.at[i], sem_b.at[i]).wait()
            base = (start ^ (2 * layer)) * 128
            for half in range(2):
                high, low = split(held_b[i, half])
                rows = pl.ds(pl.multiple_of(base + half * 64, 64), 64)
                qh[rows, :] = high
                ql[rows, :] = low

    for h in range(4):
        cols = slice(h * 256, h * 256 + 256)
        done[step, h] = product(yh[...], yl[...], qh[:, cols], ql[:, cols])

    order = (3 * layer, layer + 1, 2 - layer, 3 - 3 * layer, 3 - 3 * layer)

    def leave(s, *targets):
        for n, target in enumerate(targets):
            pltpu.make_async_copy(done.at[s, order[n]], target, sem_out.at[s, n]).start()

    for s in range(2):

        @pl.when(step == s)
        def _(s=s):
            if moving:
                d_down, d_up, w_down, w_up, beside = outs
                d, w = ((d_down, w_down), (d_up, w_up))[s]
                leave(s, w, beside.at[s], d.at[0], d.at[1])
            else:
                straight, across, still, beside = outs
                leave(s, still.at[s], beside.at[s], straight.at[s], across.at[s], beside.at[2 + s])

    @pl.when(step == 1)
    def _():
        for s in range(2):
            for n in range(4 if moving else 5):
                pltpu.make_async_copy(done.at[s, 0], outs[0].at[0], sem_out.at[s, n]).wait()


def late_product(moving, where, pieces, crossed, y, own, other):
    one = jax.ShapeDtypeStruct((512, 256), F32)
    two = jax.ShapeDtypeStruct((2, 512, 256), F32)
    four = jax.ShapeDtypeStruct((4, 512, 256), F32)
    shapes = [two, two, one, one, two] if moving else [two, two, two, four]

    def kernel(where, *refs):
        late_kernel(moving, where, *refs)

    def pair_of(step, w):
        return slot_of(moving, step, w[0]) // 2

    return pl.pallas_call(
        kernel,
        grid_spec=pltpu.PrefetchScalarGridSpec(
            num_scalar_prefetch=1,
            grid=(2,),
            in_specs=[ANYWHERE] * 16
            + [pl.BlockSpec((512, 1024), lambda s, w: (slot_of(moving, s, w[0]), 0))]
            + matrix_pieces(LATE, pair_of),
            out_specs=[ANYWHERE] * len(shapes),
            scratch_shapes=[
                pltpu.VMEM((4, 2, 2, 64, 1024), F32),
                pltpu.VMEM((8, 2, 64, 1024), F32),
                pltpu.VMEM((512, 512), BF16),
                pltpu.VMEM((512, 512), BF16),
                pltpu.VMEM((512, 1024), BF16),
                pltpu.VMEM((512, 1024), BF16),
                pltpu.VMEM((512, 1024), BF16),
                pltpu.VMEM((512, 1024), BF16),
                pltpu.VMEM((1024, 1024), BF16),
                pltpu.VMEM((1024, 1024), BF16),
                pltpu.VMEM((2, 4, 512, 256), F32),
                pltpu.SemaphoreType.DMA((4,)),
                pltpu.SemaphoreType.DMA((8,)),
                pltpu.SemaphoreType.DMA((2, 5)),
            ],
        ),
        out_shape=shapes,
        compiler_params=pltpu.CompilerParams(vmem_limit_bytes=VMEM_LIMIT),
        cost_estimate=pl.CostEstimate(
            flops=3 * 2 * 1024 * 1024 * (512 + 1024), bytes_accessed=24 << 20, transcendentals=0
        ),
        name="late_moving" if moving else "late_other",
    )(where, *pieces, *crossed, y, *[own] * 4, *[other[m] for n in range(4) for m in range(2)])


def fill_kernel(out_rows, choose, count, where, *refs):
    sources = refs[:count]
    out_ref, held, packed, in_sem, out_sem = refs[-5:]
    chosen = choose(where, sources)
    for k in range(2):
        for j in range(4):
            for condition, source in chosen[k][j]:

                @pl.when(condition)
                def _(source=source, k=k, j=j):
                    pltpu.make_async_copy(source, held.at[k, j], in_sem.at[k, j]).start()

    leaving = []
    for k in range(2):
        for j in range(4):
            pltpu.make_async_copy(chosen[k][j][0][1], held.at[k, j], in_sem.at[k, j]).wait()
            packed[k, :, j, :] = held[k, j]
        copy = pltpu.make_async_copy(packed.at[k], out_ref.at[out_rows[k]], out_sem.at[k])
        copy.start()
        leaving.append(copy)
    for copy in leaving:
        copy.wait()


def fill_rows(out_rows, choose, where, sources, previous):
    extra = [] if previous is None else [previous]
    count = len(sources)
    anywhere = pl.BlockSpec(memory_space=pl.ANY)

    def kernel(where, *refs):
        fill_kernel(out_rows, choose, count, where, *refs)

    return pl.pallas_call(
        kernel,
        grid_spec=pltpu.PrefetchScalarGridSpec(
            num_scalar_prefetch=1,
            grid=(1,),
            in_specs=[anywhere] * (count + len(extra)),
            out_specs=anywhere,
            scratch_shapes=[
                pltpu.VMEM((2, 4, 512, 256), F32),
                pltpu.VMEM((2, 512, 4, 256), F32),
                pltpu.SemaphoreType.DMA((2, 4)),
                pltpu.SemaphoreType.DMA((2,)),
            ],
        ),
        out_shape=jax.ShapeDtypeStruct((4, 512, 4, 256), F32),
        input_output_aliases={1 + count: 0} if extra else {},
        compiler_params=pltpu.CompilerParams(vmem_limit_bytes=VMEM_LIMIT),
        cost_estimate=pl.CostEstimate(flops=0, bytes_accessed=8 << 20, transcendentals=0),
        name="fill_rows",
    )(where, *sources, *extra)


def upward(r, c, l):
    if l == 0:
        return r, (c & 4) | ((c + 1) & 3), l
    return (r & 4) | ((r + 1) & 3), c, l


def downward(r, c, l):
    if l == 0:
        return r, (c & 4) | ((c + 3) & 3), l
    return (r & 4) | ((r + 3) & 3), c, l


def first_hop(r, c, l):
    return (r, c ^ 4, l) if l == 0 else (c, r, l)


def first_hop_across(r, c, l):
    return (c, r, 1) if l == 0 else (r, c ^ 4, 0)


def second_hop(r, c, l):
    return (r ^ 4, c, l) if l == 1 else (r, c, l)


def row_up(r, c, l):
    return (r + 1) & 7, c, l


def row_down(r, c, l):
    return (r + 7) & 7, c, l


def column_straight(r, c, l):
    if (c, l) in ((0, 0), (7, 1)):
        return r, c, 1 - l
    return r, c + (1 if l else -1), l


def column_across(r, c, l):
    if (c, l) in ((0, 0), (7, 1)):
        return r, c, l
    return r, c + (1 if l else -1), 1 - l


def ring_straight(r, c, l):
    return r, (c & 4) | ((c + (1 if l else 3)) & 3), l


def ring_across(r, c, l):
    return r, (c & 4) | ((c + (1 if l else 3)) & 3), 1 - l


def ring_change(r, c, l):
    return (r, c ^ 4, l) if c in (0, 7) else None


def shards(matrix, transforms):
    barrier = lax.optimization_barrier
    row_pos = lax.axis_index("row")
    col_pos = lax.axis_index("col")
    layer_pos = lax.axis_index("layer")
    where = jnp.stack([row_pos, col_pos, layer_pos]).astype(jnp.int32)
    mine = transforms[0]

    lower = layer_pos == 0
    hop = send(mine, first_hop)
    hop_across = send(mine, first_hop_across)
    beside = in_chip(mine)
    hop, hop_across, beside, mine = barrier((hop, hop_across, beside, mine))
    block = jnp.stack([jnp.where(lower, mine, beside), jnp.where(lower, beside, mine)])
    hop = jnp.stack([jnp.where(lower, hop, hop_across), jnp.where(lower, hop_across, hop)])
    own = matrix.transpose(2, 0, 1, 3).reshape(4, 2048, 256)
    away = lax.dynamic_slice_in_dim(own, 2 * (1 - layer_pos), 2, 0)
    other = [in_chip(away[m]) for m in range(2)]
    start = jnp.where(lower, block, hop)
    up = send(start, upward)
    down = send(start, downward)
    far_side = send(hop, second_hop)
    start, up, down, far_side = barrier((start, up, down, far_side))
    partner = jnp.where(lower, hop, far_side)
    partner_up = send(partner, upward)
    partner_down = send(partner, downward)
    crossed = {i: in_chip(x) for i, x in zip(EARLY, (start, partner, up, down))}
    up, partner_up, partner_down, *early = barrier(
        (up, partner_up, partner_down, *[crossed[i] for i in EARLY])
    )
    crossed = dict(zip(EARLY, early))
    far = send(up, upward)
    partner_far = send(partner_down, downward)
    y = early_product(
        where,
        [start, partner, up, None, down],
        [crossed.get(i) for i in range(5)],
        own,
        other,
    )
    crossed[3], crossed[5] = in_chip(partner_up), in_chip(partner_down)
    far, partner_far, y, crossed[3], crossed[5] = barrier(
        (far, partner_far, y, crossed[3], crossed[5])
    )
    crossed[6], crossed[7] = in_chip(far), in_chip(partner_far)
    pieces = [start, partner, up, partner_up, down, partner_down, far, partner_far]
    crossed = [crossed[i] for i in range(8)]
    d_down, d_up, w_down, w_up, beside = late_product(
        True, where, pieces, crossed, y, own, other
    )
    got_up = send(d_up, row_up)
    got_down = send(d_down, row_down)
    from_beside = in_chip(beside)
    straight, across, still, still_beside = late_product(
        False, where, pieces, crossed, y, own, other
    )
    got_up, got_down, straight, across = barrier((got_up, got_down, straight, across))
    edge_up = jnp.stack([w_up, from_beside[1]])
    edge_down = jnp.stack([w_down, from_beside[0]])
    got_straight = send(straight, ring_straight)
    got_across = send(across, ring_across)
    edge_up, edge_down, got_up, got_down = barrier((edge_up, edge_down, got_up, got_down))
    still_got_up = send(edge_up, row_up)
    still_got_down = send(edge_down, row_down)

    top = jnp.where(row_pos == 0, d_down, got_up)
    bottom = jnp.where(row_pos == 7, d_up, got_down)
    inside = jnp.where(lower, col_pos > 0, col_pos < 7)
    then_straight = jnp.stack([jnp.where(inside, x[0], x[1]) for x in (top, bottom)])
    then_across = jnp.stack([jnp.where(inside, x[1], x[0]) for x in (top, bottom)])
    then_got_straight = send(then_straight, column_straight)
    then_got_across = send(then_across, column_across)
    from_still = in_chip(still_beside)
    got_straight, got_across, then_straight = barrier((got_straight, got_across, then_straight))
    changing = jnp.where((col_pos == 0) == lower, got_across, got_straight)
    changed = send(changing, ring_change)

    def blocks(w, own, partner, moving, moving_beside, came_straight, came_across, came_changed):
        c, l = w[1], w[2]

        def both(condition, if_lower, if_upper):
            return [
                (condition & (l == which) & also, ref)
                for which, refs in ((0, if_lower), (1, if_upper))
                for also, ref in refs
            ]

        yes = c >= 0
        far_up = c == (4 if came_changed is not None else -1)
        far_down = c == (3 if came_changed is not None else -1)
        first = both((c > 0) & ~far_up, [(yes, came_across)], [(yes, came_straight)])
        last = both((c < 7) & ~far_down, [(yes, came_straight)], [(yes, came_across)])
        if came_changed is not None:
            first.append((far_up, came_changed))
            last.append((far_down, came_changed))
        return [
            first + both(c == 0, own, partner),
            both(yes, partner, own),
            both(c > 0, own, partner) + both(c == 0, [(yes, moving)], [(yes, moving_beside)]),
            last + both(c == 7, [(yes, moving_beside)], [(yes, moving)]),
        ]

    def choose_stay(w, refs):
        still, beside, straight, came_straight, came_across, came_changed = refs
        yes = w[1] >= 0
        return [
            blocks(
                w,
                [(yes, still.at[k])],
                [(yes, beside.at[k])],
                straight.at[k],
                beside.at[2 + k],
                came_straight.at[k],
                came_across.at[k],
                came_changed.at[k],
            )
            for k in range(2)
        ]

    out = fill_rows(
        (1, 2),
        choose_stay,
        where,
        [still, from_still, straight, got_straight, got_across, changed],
        None,
    )

    def choose_moved(w, refs):
        edge_up, edge_down, from_up, from_down, kept, came_straight, came_across = refs
        r = w[0]
        rows = [
            lambda n: [(r > 0, from_up.at[n]), (r == 0, edge_down.at[n])],
            lambda n: [(r < 7, from_down.at[n]), (r == 7, edge_up.at[n])],
        ]
        return [
            blocks(
                w,
                rows[k](0),
                rows[k](1),
                kept.at[k],
                came_straight.at[k],
                came_straight.at[k],
                came_across.at[k],
                None,
            )
            for k in range(2)
        ]

    return fill_rows(
        (0, 3),
        choose_moved,
        where,
        [
            edge_up,
            edge_down,
            still_got_up,
            still_got_down,
            then_across,
            then_got_straight,
            then_got_across,
        ],
        out,
    )


def solution(mesh):
    return jax.shard_map(
        shards,
        mesh=mesh,
        in_specs=(P("row", None, "col", "layer"), P(None, "row", ("col", "layer"), None)),
        out_specs=P("row", None, "col", "layer"),
        check_vma=False,
    )
```

```python
import jax
import jax.numpy as jnp
from jax import lax
from jax.experimental import pallas as pl
from jax.experimental.pallas import tpu as pltpu
from jax.sharding import PartitionSpec as P

F32 = jnp.float32
BF16 = jnp.bfloat16
AXES = ("row", "col", "layer")
VMEM_LIMIT = 58 * 1024 * 1024
EARLY = (0, 1, 2, 4)
LATE = (3, 5, 6, 7)
ANYWHERE = pl.BlockSpec(memory_space=pl.ANY)


def route(place):
    pairs = []
    for r in range(8):
        for c in range(8):
            for l in range(2):
                to = place(r, c, l)
                if to is not None:
                    pairs.append(((r * 8 + c) * 2 + l, (to[0] * 8 + to[1]) * 2 + to[2]))
    return pairs


def send(x, place):
    return lax.ppermute(x, AXES, route(place))


def in_chip(x):
    return lax.ppermute(x, "layer", [(0, 1), (1, 0)])


def split(x):
    high = x.astype(BF16)
    return high, (x - high.astype(F32)).astype(BF16)


def product(ah, al, bh, bl):
    def dot(a, b):
        return jnp.dot(a, b, preferred_element_type=F32)

    return dot(ah, bh) + (dot(ah, bl) + dot(al, bh))


def holders(i):
    up = (i & 4) | ((i + 3) & 3)
    down = (i & 4) | ((i + 1) & 3)
    far = (i & 4) | ((i + 2) & 3)
    return [i, i ^ 4, up, up ^ 4, down, down ^ 4, far, far ^ 4]


def turned(ref, index, pair, cols):
    rows = jnp.concatenate([ref[index, 0, pair, :, cols], ref[index, 1, pair, :, cols]], axis=0)
    return split(rows.T)


def halves_of_matrix(own_refs, other_refs, mh, ml):
    for n in range(4):
        for m in range(2):
            for k, block in enumerate((own_refs[n][m], other_refs[2 * n + m][...])):
                high, low = split(block)
                lanes = slice(m * 512 + k * 256, m * 512 + k * 256 + 256)
                mh[n * 128 : n * 128 + 128, lanes] = high
                ml[n * 128 : n * 128 + 128, lanes] = low


def early_kernel(where, *refs):
    ours, theirs = refs[:4], refs[4:8]
    own_refs, other_refs = refs[8:12], refs[12:20]
    y_ref, held, jh, jl, mh, ml, sem = refs[20:]
    pair = pl.program_id(0)
    layer = where[2]

    @pl.when(pair == 0)
    def _():
        for i in range(4):

            @pl.when(layer == 0)
            def _(i=i):
                pltpu.make_async_copy(ours[i], held.at[i], sem.at[i]).start()

            @pl.when(layer == 1)
            def _(i=i):
                pltpu.make_async_copy(theirs[i], held.at[i], sem.at[i]).start()

    halves_of_matrix(own_refs, other_refs, mh, ml)

    @pl.when(pair == 0)
    def _():
        for i in range(4):
            pltpu.make_async_copy(ours[i], held.at[i], sem.at[i]).wait()

    for i in range(4):
        for half in range(4):
            high, low = turned(held, i, pair, pl.ds(half * 256, 256))
            jh[half * 256 : half * 256 + 256, i * 128 : i * 128 + 128] = high
            jl[half * 256 : half * 256 + 256, i * 128 : i * 128 + 128] = low
    for a in range(4):
        rows = pl.ds(a * 256, 256)
        y_ref[rows, :] = product(jh[rows, :], jl[rows, :], mh[...], ml[...])


def matrix_pieces(which, pair_of):
    def rows(i):
        return lambda step, w: pair_of(step, w) * 8 + holders(w[1])[i]

    own = [pl.BlockSpec((2, 128, 256), lambda s, w, f=rows(i): (w[2], f(s, w), 0)) for i in which]
    other = [pl.BlockSpec((128, 256), lambda s, w, f=rows(i): (f(s, w), 0)) for i in which]
    return own + [spec for spec in other for m in range(2)]


def early_product(where, pieces, crossed, own, other):
    return pl.pallas_call(
        early_kernel,
        grid_spec=pltpu.PrefetchScalarGridSpec(
            num_scalar_prefetch=1,
            grid=(2,),
            in_specs=[ANYWHERE] * 8 + matrix_pieces(EARLY, lambda p, w: p),
            out_specs=pl.BlockSpec((1024, 1024), lambda p, w: (p, 0)),
            scratch_shapes=[
                pltpu.VMEM((4, 2, 2, 64, 1024), F32),
                pltpu.VMEM((1024, 512), BF16),
                pltpu.VMEM((1024, 512), BF16),
                pltpu.VMEM((512, 1024), BF16),
                pltpu.VMEM((512, 1024), BF16),
                pltpu.SemaphoreType.DMA((4,)),
            ],
        ),
        out_shape=jax.ShapeDtypeStruct((2048, 1024), F32),
        compiler_params=pltpu.CompilerParams(vmem_limit_bytes=VMEM_LIMIT),
        cost_estimate=pl.CostEstimate(
            flops=3 * 2 * 2048 * 512 * 1024, bytes_accessed=24 << 20, transcendentals=0
        ),
        name="early_product",
    )(
        where,
        *[pieces[i] for i in EARLY],
        *[crossed[i] for i in EARLY],
        *[own] * 4,
        *[other[m] for n in range(4) for m in range(2)],
    )


def by_role(slot, row_pos, down, up, stays):
    for s, condition, action in (
        (0, row_pos == 0, down),
        (0, row_pos > 0, lambda s: stays(s, 1)),
        (1, row_pos == 0, lambda s: stays(s, 1)),
        (1, row_pos > 0, down),
        (2, row_pos >= 0, up),
        (3, row_pos >= 0, lambda s: stays(s, 0)),
    ):

        @pl.when((slot == s) & condition)
        def _(s=s, action=action):
            action(s)


def fetch_columns(layer, ours, theirs, lane, held, sem):
    for core, sources in ((0, theirs), (1, ours)):

        @pl.when(layer == core)
        def _(core=core, sources=sources):
            for i in range(8):
                source = sources[i].at[:, core, :, pl.ds(lane(core) * 512, 512)]
                pltpu.make_async_copy(source, held.at[i], sem.at[i]).start()


def take_columns(row_pos, layer, held, sem, qh, ql):
    for i, start in enumerate(holders(row_pos)):
        pltpu.make_async_copy(held.at[i], held.at[i], sem.at[i]).wait()
        base = (start ^ (2 * layer)) * 128
        for half in range(2):
            high, low = split(held[i, half])
            rows = pl.ds(pl.multiple_of(base + half * 64, 64), 64)
            qh[rows, :] = high
            ql[rows, :] = low


def moving_kernel(where, *refs):
    ours, theirs = refs[:8], refs[8:16]
    y_ref = refs[16]
    own_refs, other_refs = refs[17:21], refs[21:29]
    yh, yl, d_down, d_up, straight, across = refs[29:35]
    held_a, held_b, jh, jl, mh, ml, qh, ql, done, sem_a, sem_b, sem_out = refs[35:]
    slot = pl.program_id(0)
    row_pos, layer = where[0], where[2]
    pair = slot // 2

    @pl.when(slot == 0)
    def _():
        for core, sources in ((0, ours), (1, theirs)):

            @pl.when(layer == core)
            def _(sources=sources):
                for n, i in enumerate(LATE):
                    pltpu.make_async_copy(sources[i], held_a.at[n], sem_a.at[n]).start()

        fetch_columns(layer, ours, theirs, lambda core: 1 - core, held_b, sem_b)

    @pl.when(slot % 2 == 0)
    def _():
        halves_of_matrix(own_refs, other_refs, mh, ml)

    @pl.when(slot == 0)
    def _():
        for n, i in enumerate(LATE):
            pltpu.make_async_copy(ours[i], held_a.at[n], sem_a.at[n]).wait()

    for n in range(4):
        for a in range(2):
            cols = pl.ds(pl.multiple_of((slot % 2) * 512 + a * 256, 256), 256)
            high, low = turned(held_a, n, pair, cols)
            jh[a * 256 : a * 256 + 256, n * 128 : n * 128 + 128] = high
            jl[a * 256 : a * 256 + 256, n * 128 : n * 128 + 128] = low

    for h in range(2):
        cols = slice(h * 512, h * 512 + 512)
        high, low = split(y_ref[:, cols] + product(jh[...], jl[...], mh[:, cols], ml[:, cols]))
        yh[:, cols] = high
        yl[:, cols] = low

    @pl.when(slot == 0)
    def _():
        take_columns(row_pos, layer, held_b, sem_b, qh, ql)

    for h in range(2):
        cols = slice(h * 256, h * 256 + 256)
        done[slot, h] = product(yh[...], yl[...], qh[:, cols], ql[:, cols])

    def leave(s, near, far):
        pltpu.make_async_copy(done.at[s, layer], near, sem_out.at[s, 0]).start()
        pltpu.make_async_copy(done.at[s, 1 - layer], far, sem_out.at[s, 1]).start()

    by_role(
        slot,
        row_pos,
        lambda s: leave(s, d_down.at[0], d_down.at[1]),
        lambda s: leave(s, d_up.at[0], d_up.at[1]),
        lambda s, k: leave(s, straight.at[k], across.at[k]),
    )

    @pl.when(slot == 3)
    def _():
        for s in range(4):
            for n in range(2):
                pltpu.make_async_copy(done.at[s, n], d_up.at[n], sem_out.at[s, n]).wait()


def still_kernel(where, *refs):
    ours, theirs = refs[:8], refs[8:16]
    yh, yl = refs[16:18]
    w_down, w_up, still, beside = refs[18:22]
    held_b, qh, ql, done, sem_b, sem_out = refs[22:]
    slot = pl.program_id(0)
    row_pos, layer = where[0], where[2]

    @pl.when(slot == 0)
    def _():
        fetch_columns(layer, ours, theirs, lambda core: core, held_b, sem_b)
        take_columns(row_pos, layer, held_b, sem_b, qh, ql)

    for h in range(2):
        cols = slice(h * 256, h * 256 + 256)
        done[slot, h] = product(yh[...], yl[...], qh[:, cols], ql[:, cols])

    def leave(s, near, far):
        pltpu.make_async_copy(done.at[s, layer], near, sem_out.at[s, 0]).start()
        pltpu.make_async_copy(done.at[s, 1 - layer], far, sem_out.at[s, 1]).start()

    by_role(
        slot,
        row_pos,
        lambda s: leave(s, w_down, beside.at[2]),
        lambda s: leave(s, w_up, beside.at[3]),
        lambda s, k: leave(s, still.at[k], beside.at[k]),
    )

    @pl.when(slot == 3)
    def _():
        for s in range(4):
            for n in range(2):
                pltpu.make_async_copy(done.at[s, n], w_up, sem_out.at[s, n]).wait()


ONE = jax.ShapeDtypeStruct((512, 256), F32)
TWO = jax.ShapeDtypeStruct((2, 512, 256), F32)
FOUR = jax.ShapeDtypeStruct((4, 512, 256), F32)
HALF = jax.ShapeDtypeStruct((2048, 1024), BF16)


def moving_product(where, pieces, crossed, y, own, other):
    block = pl.BlockSpec((512, 1024), lambda s, w: (s, 0))
    return pl.pallas_call(
        moving_kernel,
        grid_spec=pltpu.PrefetchScalarGridSpec(
            num_scalar_prefetch=1,
            grid=(4,),
            in_specs=[ANYWHERE] * 16 + [block] + matrix_pieces(LATE, lambda s, w: s // 2),
            out_specs=[block] * 2 + [ANYWHERE] * 4,
            scratch_shapes=[
                pltpu.VMEM((4, 2, 2, 64, 1024), F32),
                pltpu.VMEM((8, 2, 64, 512), F32),
                pltpu.VMEM((512, 512), BF16),
                pltpu.VMEM((512, 512), BF16),
                pltpu.VMEM((512, 1024), BF16),
                pltpu.VMEM((512, 1024), BF16),
                pltpu.VMEM((1024, 512), BF16),
                pltpu.VMEM((1024, 512), BF16),
                pltpu.VMEM((4, 2, 512, 256), F32),
                pltpu.SemaphoreType.DMA((4,)),
                pltpu.SemaphoreType.DMA((8,)),
                pltpu.SemaphoreType.DMA((4, 2)),
            ],
        ),
        out_shape=[HALF] * 2 + [TWO] * 4,
        compiler_params=pltpu.CompilerParams(vmem_limit_bytes=VMEM_LIMIT),
        cost_estimate=pl.CostEstimate(
            flops=3 * 2 * 2048 * 1024 * (512 + 512), bytes_accessed=36 << 20, transcendentals=0
        ),
        name="moving_product",
    )(where, *pieces, *crossed, y, *[own] * 4, *[other[m] for n in range(4) for m in range(2)])


def still_product(where, pieces, crossed, yh, yl):
    block = pl.BlockSpec((512, 1024), lambda s, w: (s, 0))
    return pl.pallas_call(
        still_kernel,
        grid_spec=pltpu.PrefetchScalarGridSpec(
            num_scalar_prefetch=1,
            grid=(4,),
            in_specs=[ANYWHERE] * 16 + [block] * 2,
            out_specs=[ANYWHERE] * 4,
            scratch_shapes=[
                pltpu.VMEM((8, 2, 64, 512), F32),
                pltpu.VMEM((1024, 512), BF16),
                pltpu.VMEM((1024, 512), BF16),
                pltpu.VMEM((4, 2, 512, 256), F32),
                pltpu.SemaphoreType.DMA((8,)),
                pltpu.SemaphoreType.DMA((4, 2)),
            ],
        ),
        out_shape=[ONE, ONE, TWO, FOUR],
        compiler_params=pltpu.CompilerParams(vmem_limit_bytes=VMEM_LIMIT),
        cost_estimate=pl.CostEstimate(
            flops=3 * 2 * 2048 * 1024 * 512, bytes_accessed=20 << 20, transcendentals=0
        ),
        name="still_product",
    )(where, *pieces, *crossed, yh, yl)


def fill_kernel(out_rows, choose, count, where, *refs):
    sources = refs[:count]
    out_ref, held, packed, in_sem, out_sem = refs[-5:]
    chosen = choose(where, sources)
    for k in range(2):
        for j in range(4):
            for condition, source in chosen[k][j]:

                @pl.when(condition)
                def _(source=source, k=k, j=j):
                    pltpu.make_async_copy(source, held.at[k, j], in_sem.at[k, j]).start()

    leaving = []
    for k in range(2):
        for j in range(4):
            pltpu.make_async_copy(chosen[k][j][0][1], held.at[k, j], in_sem.at[k, j]).wait()
            packed[k, :, j, :] = held[k, j]
        copy = pltpu.make_async_copy(packed.at[k], out_ref.at[out_rows[k]], out_sem.at[k])
        copy.start()
        leaving.append(copy)
    for copy in leaving:
        copy.wait()


def fill_rows(out_rows, choose, where, sources, previous):
    extra = [] if previous is None else [previous]
    count = len(sources)
    anywhere = pl.BlockSpec(memory_space=pl.ANY)

    def kernel(where, *refs):
        fill_kernel(out_rows, choose, count, where, *refs)

    return pl.pallas_call(
        kernel,
        grid_spec=pltpu.PrefetchScalarGridSpec(
            num_scalar_prefetch=1,
            grid=(1,),
            in_specs=[anywhere] * (count + len(extra)),
            out_specs=anywhere,
            scratch_shapes=[
                pltpu.VMEM((2, 4, 512, 256), F32),
                pltpu.VMEM((2, 512, 4, 256), F32),
                pltpu.SemaphoreType.DMA((2, 4)),
                pltpu.SemaphoreType.DMA((2,)),
            ],
        ),
        out_shape=jax.ShapeDtypeStruct((4, 512, 4, 256), F32),
        input_output_aliases={1 + count: 0} if extra else {},
        compiler_params=pltpu.CompilerParams(vmem_limit_bytes=VMEM_LIMIT),
        cost_estimate=pl.CostEstimate(flops=0, bytes_accessed=8 << 20, transcendentals=0),
        name="fill_rows",
    )(where, *sources, *extra)


def upward(r, c, l):
    if l == 0:
        return r, (c & 4) | ((c + 1) & 3), l
    return (r & 4) | ((r + 1) & 3), c, l


def downward(r, c, l):
    if l == 0:
        return r, (c & 4) | ((c + 3) & 3), l
    return (r & 4) | ((r + 3) & 3), c, l


def first_hop(r, c, l):
    return (r, c ^ 4, l) if l == 0 else (c, r, l)


def first_hop_across(r, c, l):
    return (c, r, 1) if l == 0 else (r, c ^ 4, 0)


def second_hop(r, c, l):
    return (r ^ 4, c, l) if l == 1 else None


def row_up(r, c, l):
    return (r + 1) & 7, c, l


def row_down(r, c, l):
    return (r + 7) & 7, c, l


def column_straight(r, c, l):
    if (c, l) in ((0, 0), (7, 1)):
        return r, c, 1 - l
    return r, c + (1 if l else -1), l


def column_across(r, c, l):
    if (c, l) in ((0, 0), (7, 1)):
        return r, c, l
    return r, c + (1 if l else -1), 1 - l


def ring_straight(r, c, l):
    return r, (c & 4) | ((c + (1 if l else 3)) & 3), l


def ring_across(r, c, l):
    return r, (c & 4) | ((c + (1 if l else 3)) & 3), 1 - l


def ring_change(r, c, l):
    return (r, c ^ 4, l) if c in (0, 7) else None


def shards(matrix, transforms):
    barrier = lax.optimization_barrier
    row_pos = lax.axis_index("row")
    col_pos = lax.axis_index("col")
    layer_pos = lax.axis_index("layer")
    where = jnp.stack([row_pos, col_pos, layer_pos]).astype(jnp.int32)
    mine = transforms[0]

    lower = layer_pos == 0
    hop = send(mine, first_hop)
    hop_across = send(mine, first_hop_across)
    beside = in_chip(mine)
    hop, hop_across, beside, mine = barrier((hop, hop_across, beside, mine))
    block = jnp.stack([jnp.where(lower, mine, beside), jnp.where(lower, beside, mine)])
    hop = jnp.stack([jnp.where(lower, hop, hop_across), jnp.where(lower, hop_across, hop)])
    own = matrix.transpose(2, 0, 1, 3).reshape(4, 2048, 256)
    away = lax.dynamic_slice_in_dim(own, 2 * (1 - layer_pos), 2, 0)
    other = [in_chip(away[m]) for m in range(2)]
    start = jnp.where(lower, block, hop)
    up = send(start, upward)
    down = send(start, downward)
    far_side = send(hop, second_hop)
    start, up, down, far_side = barrier((start, up, down, far_side))
    partner = jnp.where(lower, hop, far_side)
    partner_up = send(partner, upward)
    partner_down = send(partner, downward)
    crossed = {i: in_chip(x) for i, x in zip(EARLY, (start, partner, up, down))}
    up, partner_up, partner_down, *early = barrier(
        (up, partner_up, partner_down, *[crossed[i] for i in EARLY])
    )
    crossed = dict(zip(EARLY, early))
    far = send(up, upward)
    partner_far = send(partner_down, downward)
    y = early_product(
        where,
        [start, partner, up, None, down],
        [crossed.get(i) for i in range(5)],
        own,
        other,
    )
    crossed[3], crossed[5] = in_chip(partner_up), in_chip(partner_down)
    far, partner_far, y, crossed[3], crossed[5] = barrier(
        (far, partner_far, y, crossed[3], crossed[5])
    )
    crossed[6], crossed[7] = in_chip(far), in_chip(partner_far)
    pieces = [start, partner, up, partner_up, down, partner_down, far, partner_far]
    crossed = [crossed[i] for i in range(8)]
    yh, yl, d_down, d_up, straight, across = moving_product(
        where, pieces, crossed, y, own, other
    )
    got_up = send(d_up, row_up)
    got_down = send(d_down, row_down)
    got_straight = send(straight, ring_straight)
    got_across = send(across, ring_across)
    across_beside = in_chip(across)
    w_down, w_up, still, beside = still_product(where, pieces, crossed, yh, yl)
    got_up, got_down, got_straight, got_across, across_beside, w_down, w_up, still, beside = barrier(
        (got_up, got_down, got_straight, got_across, across_beside, w_down, w_up, still, beside)
    )
    changed = send(jnp.where((col_pos == 0) == lower, got_across, got_straight), ring_change)
    from_still = in_chip(beside)
    edge_up = jnp.stack([w_up, from_still[3]])
    edge_down = jnp.stack([w_down, from_still[2]])
    still_got_up = send(edge_up, row_up)
    still_got_down = send(edge_down, row_down)

    top = jnp.where(row_pos == 0, d_down, got_up)
    bottom = jnp.where(row_pos == 7, d_up, got_down)
    inside = jnp.where(lower, col_pos > 0, col_pos < 7)
    then_straight = jnp.stack([jnp.where(inside, x[0], x[1]) for x in (top, bottom)])
    then_across = jnp.stack([jnp.where(inside, x[1], x[0]) for x in (top, bottom)])
    then_got_straight = send(then_straight, column_straight)
    then_got_across = send(then_across, column_across)
    def blocks(w, own, partner, kept, kept_beside, came_straight, came_across, came_changed):
        c, l = w[1], w[2]

        def both(condition, if_lower, if_upper):
            return [
                (condition & (l == which) & also, ref)
                for which, refs in ((0, if_lower), (1, if_upper))
                for also, ref in refs
            ]

        yes = c >= 0
        kept, kept_beside = [(yes, kept)], [(yes, kept_beside)]
        straight, across = [(yes, came_straight)], [(yes, came_across)]
        if came_changed is None:
            first, last = both(c > 0, across, straight), both(c < 7, straight, across)
        else:
            first = both((c > 0) & (c != 4), across, straight) + [(c == 4, came_changed)]
            last = both((c < 7) & (c != 3), straight, across) + [(c == 3, came_changed)]
        return [
            first + both(c == 0, own, partner),
            both(yes, partner, own),
            both(c > 0, own, partner) + both(c == 0, kept, kept_beside),
            last + both(c == 7, kept_beside, kept),
        ]

    def choose_stay(w, refs):
        still, beside, kept, kept_beside, came_straight, came_across, came_changed = refs
        yes = w[1] >= 0
        return [
            blocks(
                w,
                [(yes, still.at[k])],
                [(yes, beside.at[k])],
                kept.at[k],
                kept_beside.at[k],
                came_straight.at[k],
                came_across.at[k],
                came_changed.at[k],
            )
            for k in range(2)
        ]

    out = fill_rows(
        (1, 2),
        choose_stay,
        where,
        [still, from_still, straight, across_beside, got_straight, got_across, changed],
        None,
    )

    def choose_moved(w, refs):
        edge_up, edge_down, from_up, from_down, kept, came_straight, came_across = refs
        r = w[0]
        rows = [
            lambda n: [(r > 0, from_up.at[n]), (r == 0, edge_down.at[n])],
            lambda n: [(r < 7, from_down.at[n]), (r == 7, edge_up.at[n])],
        ]
        return [
            blocks(
                w,
                rows[k](0),
                rows[k](1),
                kept.at[k],
                came_straight.at[k],
                came_straight.at[k],
                came_across.at[k],
                None,
            )
            for k in range(2)
        ]

    return fill_rows(
        (0, 3),
        choose_moved,
        where,
        [
            edge_up,
            edge_down,
            still_got_up,
            still_got_down,
            then_across,
            then_got_straight,
            then_got_across,
        ],
        out,
    )


def solution(mesh):
    return jax.shard_map(
        shards,
        mesh=mesh,
        in_specs=(P("row", None, "col", "layer"), P(None, "row", ("col", "layer"), None)),
        out_specs=P("row", None, "col", "layer"),
        check_vma=False,
    )
```

```python
import jax
import jax.numpy as jnp
from jax import lax
from jax.experimental import pallas as pl
from jax.experimental.pallas import tpu as pltpu
from jax.sharding import PartitionSpec as P

F32 = jnp.float32
BF16 = jnp.bfloat16
AXES = ("row", "col", "layer")
VMEM_LIMIT = 58 * 1024 * 1024
EARLY = (0, 1, 2, 4)
LATE = (3, 5, 6, 7)
ANYWHERE = pl.BlockSpec(memory_space=pl.ANY)


def route(place):
    pairs = []
    for r in range(8):
        for c in range(8):
            for l in range(2):
                to = place(r, c, l)
                if to is not None:
                    pairs.append(((r * 8 + c) * 2 + l, (to[0] * 8 + to[1]) * 2 + to[2]))
    return pairs


def send(x, place):
    return lax.ppermute(x, AXES, route(place))


def in_chip(x):
    return lax.ppermute(x, "layer", [(0, 1), (1, 0)])


def split(x):
    high = x.astype(BF16)
    return high, (x - high.astype(F32)).astype(BF16)


def product(ah, al, bh, bl):
    def dot(a, b):
        return jnp.dot(a, b, preferred_element_type=F32)

    return dot(ah, bh) + (dot(ah, bl) + dot(al, bh))


def holders(i):
    up = (i & 4) | ((i + 3) & 3)
    down = (i & 4) | ((i + 1) & 3)
    far = (i & 4) | ((i + 2) & 3)
    return [i, i ^ 4, up, up ^ 4, down, down ^ 4, far, far ^ 4]


def turned(ref, index, pair, cols):
    rows = jnp.concatenate([ref[index, 0, pair, :, cols], ref[index, 1, pair, :, cols]], axis=0)
    return split(rows.T)


def halves_of_matrix(own_refs, other_refs, mh, ml):
    for n in range(4):
        for m in range(2):
            for k, block in enumerate((own_refs[n][m], other_refs[2 * n + m][...])):
                high, low = split(block)
                lanes = slice(m * 512 + k * 256, m * 512 + k * 256 + 256)
                mh[n * 128 : n * 128 + 128, lanes] = high
                ml[n * 128 : n * 128 + 128, lanes] = low


def early_kernel(where, *refs):
    ours, theirs = refs[:4], refs[4:8]
    own_refs, other_refs = refs[8:12], refs[12:20]
    y_ref, held, jh, jl, mh, ml, sem = refs[20:]
    pair = pl.program_id(0)
    layer = where[2]

    @pl.when(pair == 0)
    def _():
        for i in range(4):

            @pl.when(layer == 0)
            def _(i=i):
                pltpu.make_async_copy(ours[i], held.at[i], sem.at[i]).start()

            @pl.when(layer == 1)
            def _(i=i):
                pltpu.make_async_copy(theirs[i], held.at[i], sem.at[i]).start()

    halves_of_matrix(own_refs, other_refs, mh, ml)

    @pl.when(pair == 0)
    def _():
        for i in range(4):
            pltpu.make_async_copy(ours[i], held.at[i], sem.at[i]).wait()

    for i in range(4):
        for half in range(4):
            high, low = turned(held, i, pair, pl.ds(half * 256, 256))
            jh[half * 256 : half * 256 + 256, i * 128 : i * 128 + 128] = high
            jl[half * 256 : half * 256 + 256, i * 128 : i * 128 + 128] = low
    for a in range(4):
        rows = pl.ds(a * 256, 256)
        y_ref[rows, :] = product(jh[rows, :], jl[rows, :], mh[...], ml[...])


def matrix_pieces(which, pair_of):
    def rows(i):
        return lambda step, w: pair_of(step, w) * 8 + holders(w[1])[i]

    own = [pl.BlockSpec((2, 128, 256), lambda s, w, f=rows(i): (w[2], f(s, w), 0)) for i in which]
    other = [pl.BlockSpec((128, 256), lambda s, w, f=rows(i): (f(s, w), 0)) for i in which]
    return own + [spec for spec in other for m in range(2)]


def early_product(where, pieces, crossed, own, other):
    return pl.pallas_call(
        early_kernel,
        grid_spec=pltpu.PrefetchScalarGridSpec(
            num_scalar_prefetch=1,
            grid=(2,),
            in_specs=[ANYWHERE] * 8 + matrix_pieces(EARLY, lambda p, w: p),
            out_specs=pl.BlockSpec((1024, 1024), lambda p, w: (p, 0)),
            scratch_shapes=[
                pltpu.VMEM((4, 2, 2, 64, 1024), F32),
                pltpu.VMEM((1024, 512), BF16),
                pltpu.VMEM((1024, 512), BF16),
                pltpu.VMEM((512, 1024), BF16),
                pltpu.VMEM((512, 1024), BF16),
                pltpu.SemaphoreType.DMA((4,)),
            ],
        ),
        out_shape=jax.ShapeDtypeStruct((2048, 1024), F32),
        compiler_params=pltpu.CompilerParams(vmem_limit_bytes=VMEM_LIMIT),
        cost_estimate=pl.CostEstimate(
            flops=3 * 2 * 2048 * 512 * 1024, bytes_accessed=24 << 20, transcendentals=0
        ),
        name="early_product",
    )(
        where,
        *[pieces[i] for i in EARLY],
        *[crossed[i] for i in EARLY],
        *[own] * 4,
        *[other[m] for n in range(4) for m in range(2)],
    )


def by_role(slot, row_pos, down, up, stays):
    for s, condition, action in (
        (0, row_pos == 0, down),
        (0, row_pos > 0, lambda s: stays(s, 1)),
        (1, row_pos == 0, lambda s: stays(s, 1)),
        (1, row_pos > 0, down),
        (2, row_pos >= 0, up),
        (3, row_pos >= 0, lambda s: stays(s, 0)),
    ):

        @pl.when((slot == s) & condition)
        def _(s=s, action=action):
            action(s)


def fetch_columns(layer, ours, theirs, lane, held, sem):
    for core, sources in ((0, theirs), (1, ours)):

        @pl.when(layer == core)
        def _(core=core, sources=sources):
            for i in range(8):
                source = sources[i].at[:, core, :, pl.ds(lane(core) * 512, 512)]
                pltpu.make_async_copy(source, held.at[i], sem.at[i]).start()


def take_columns(row_pos, layer, held, sem, qh, ql):
    for i, start in enumerate(holders(row_pos)):
        pltpu.make_async_copy(held.at[i], held.at[i], sem.at[i]).wait()
        base = (start ^ (2 * layer)) * 128
        for half in range(2):
            high, low = split(held[i, half])
            rows = pl.ds(pl.multiple_of(base + half * 64, 64), 64)
            qh[rows, :] = high
            ql[rows, :] = low


def moving_kernel(where, *refs):
    ours, theirs = refs[:8], refs[8:16]
    y_ref = refs[16]
    own_refs, other_refs = refs[17:21], refs[21:29]
    yh, yl, d_down, d_up, straight, across = refs[29:35]
    held_a, held_b, jh, jl, mh, ml, qh, ql, done, sem_a, sem_b, sem_out = refs[35:]
    slot = pl.program_id(0)
    row_pos, layer = where[0], where[2]
    pair = slot // 2

    @pl.when(slot == 0)
    def _():
        for core, sources in ((0, ours), (1, theirs)):

            @pl.when(layer == core)
            def _(sources=sources):
                for n, i in enumerate(LATE):
                    pltpu.make_async_copy(sources[i], held_a.at[n], sem_a.at[n]).start()

        fetch_columns(layer, ours, theirs, lambda core: 1 - core, held_b, sem_b)

    @pl.when(slot % 2 == 0)
    def _():
        halves_of_matrix(own_refs, other_refs, mh, ml)

    @pl.when(slot == 0)
    def _():
        for n, i in enumerate(LATE):
            pltpu.make_async_copy(ours[i], held_a.at[n], sem_a.at[n]).wait()

    for n in range(4):
        for a in range(2):
            cols = pl.ds(pl.multiple_of((slot % 2) * 512 + a * 256, 256), 256)
            high, low = turned(held_a, n, pair, cols)
            jh[a * 256 : a * 256 + 256, n * 128 : n * 128 + 128] = high
            jl[a * 256 : a * 256 + 256, n * 128 : n * 128 + 128] = low

    for h in range(2):
        cols = slice(h * 512, h * 512 + 512)
        high, low = split(y_ref[:, cols] + product(jh[...], jl[...], mh[:, cols], ml[:, cols]))
        yh[:, cols] = high
        yl[:, cols] = low

    @pl.when(slot == 0)
    def _():
        take_columns(row_pos, layer, held_b, sem_b, qh, ql)

    for h in range(2):
        cols = slice(h * 256, h * 256 + 256)
        done[slot, h] = product(yh[...], yl[...], qh[:, cols], ql[:, cols])

    def leave(s, near, far):
        pltpu.make_async_copy(done.at[s, layer], near, sem_out.at[s, 0]).start()
        pltpu.make_async_copy(done.at[s, 1 - layer], far, sem_out.at[s, 1]).start()

    by_role(
        slot,
        row_pos,
        lambda s: leave(s, d_down.at[0], d_down.at[1]),
        lambda s: leave(s, d_up.at[0], d_up.at[1]),
        lambda s, k: leave(s, straight.at[k], across.at[k]),
    )

    @pl.when(slot == 3)
    def _():
        for s in range(4):
            for n in range(2):
                pltpu.make_async_copy(done.at[s, n], d_up.at[n], sem_out.at[s, n]).wait()


def still_kernel(where, *refs):
    ours, theirs = refs[:8], refs[8:16]
    yh, yl = refs[16:18]
    w_down, w_up, still, beside = refs[18:22]
    held_b, qh, ql, done, sem_b, sem_out = refs[22:]
    slot = pl.program_id(0)
    row_pos, layer = where[0], where[2]

    @pl.when(slot == 0)
    def _():
        fetch_columns(layer, ours, theirs, lambda core: core, held_b, sem_b)
        take_columns(row_pos, layer, held_b, sem_b, qh, ql)

    for h in range(2):
        cols = slice(h * 256, h * 256 + 256)
        done[slot, h] = product(yh[...], yl[...], qh[:, cols], ql[:, cols])

    def leave(s, near, far):
        pltpu.make_async_copy(done.at[s, layer], near, sem_out.at[s, 0]).start()
        pltpu.make_async_copy(done.at[s, 1 - layer], far, sem_out.at[s, 1]).start()

    by_role(
        slot,
        row_pos,
        lambda s: leave(s, w_down, beside.at[2]),
        lambda s: leave(s, w_up, beside.at[3]),
        lambda s, k: leave(s, still.at[k], beside.at[k]),
    )

    @pl.when(slot == 3)
    def _():
        for s in range(4):
            for n in range(2):
                pltpu.make_async_copy(done.at[s, n], w_up, sem_out.at[s, n]).wait()


ONE = jax.ShapeDtypeStruct((512, 256), F32)
TWO = jax.ShapeDtypeStruct((2, 512, 256), F32)
FOUR = jax.ShapeDtypeStruct((4, 512, 256), F32)
HALF = jax.ShapeDtypeStruct((2048, 1024), BF16)


def moving_product(where, pieces, crossed, y, own, other):
    block = pl.BlockSpec((512, 1024), lambda s, w: (s, 0))
    return pl.pallas_call(
        moving_kernel,
        grid_spec=pltpu.PrefetchScalarGridSpec(
            num_scalar_prefetch=1,
            grid=(4,),
            in_specs=[ANYWHERE] * 16 + [block] + matrix_pieces(LATE, lambda s, w: s // 2),
            out_specs=[block] * 2 + [ANYWHERE] * 4,
            scratch_shapes=[
                pltpu.VMEM((4, 2, 2, 64, 1024), F32),
                pltpu.VMEM((8, 2, 64, 512), F32),
                pltpu.VMEM((512, 512), BF16),
                pltpu.VMEM((512, 512), BF16),
                pltpu.VMEM((512, 1024), BF16),
                pltpu.VMEM((512, 1024), BF16),
                pltpu.VMEM((1024, 512), BF16),
                pltpu.VMEM((1024, 512), BF16),
                pltpu.VMEM((4, 2, 512, 256), F32),
                pltpu.SemaphoreType.DMA((4,)),
                pltpu.SemaphoreType.DMA((8,)),
                pltpu.SemaphoreType.DMA((4, 2)),
            ],
        ),
        out_shape=[HALF] * 2 + [TWO] * 4,
        compiler_params=pltpu.CompilerParams(vmem_limit_bytes=VMEM_LIMIT),
        cost_estimate=pl.CostEstimate(
            flops=3 * 2 * 2048 * 1024 * (512 + 512), bytes_accessed=36 << 20, transcendentals=0
        ),
        name="moving_product",
    )(where, *pieces, *crossed, y, *[own] * 4, *[other[m] for n in range(4) for m in range(2)])


def still_product(where, pieces, crossed, yh, yl):
    block = pl.BlockSpec((512, 1024), lambda s, w: (s, 0))
    return pl.pallas_call(
        still_kernel,
        grid_spec=pltpu.PrefetchScalarGridSpec(
            num_scalar_prefetch=1,
            grid=(4,),
            in_specs=[ANYWHERE] * 16 + [block] * 2,
            out_specs=[ANYWHERE] * 4,
            scratch_shapes=[
                pltpu.VMEM((8, 2, 64, 512), F32),
                pltpu.VMEM((1024, 512), BF16),
                pltpu.VMEM((1024, 512), BF16),
                pltpu.VMEM((4, 2, 512, 256), F32),
                pltpu.SemaphoreType.DMA((8,)),
                pltpu.SemaphoreType.DMA((4, 2)),
            ],
        ),
        out_shape=[ONE, ONE, TWO, FOUR],
        compiler_params=pltpu.CompilerParams(vmem_limit_bytes=VMEM_LIMIT),
        cost_estimate=pl.CostEstimate(
            flops=3 * 2 * 2048 * 1024 * 512, bytes_accessed=20 << 20, transcendentals=0
        ),
        name="still_product",
    )(where, *pieces, *crossed, yh, yl)


def fill_kernel(out_rows, choose, count, where, *refs):
    sources = refs[:count]
    out_ref, held, packed, in_sem, out_sem = refs[-5:]
    chosen = choose(where, sources)
    for k in range(2):
        for j in range(4):
            for condition, source in chosen[k][j]:

                @pl.when(condition)
                def _(source=source, k=k, j=j):
                    pltpu.make_async_copy(source, held.at[k, j], in_sem.at[k, j]).start()

    leaving = []
    for k in range(2):
        for j in range(4):
            pltpu.make_async_copy(chosen[k][j][0][1], held.at[k, j], in_sem.at[k, j]).wait()
            packed[k, :, j, :] = held[k, j]
        copy = pltpu.make_async_copy(packed.at[k], out_ref.at[out_rows[k]], out_sem.at[k])
        copy.start()
        leaving.append(copy)
    for copy in leaving:
        copy.wait()


def fill_rows(out_rows, choose, where, sources, previous):
    extra = [] if previous is None else [previous]
    count = len(sources)
    anywhere = pl.BlockSpec(memory_space=pl.ANY)

    def kernel(where, *refs):
        fill_kernel(out_rows, choose, count, where, *refs)

    return pl.pallas_call(
        kernel,
        grid_spec=pltpu.PrefetchScalarGridSpec(
            num_scalar_prefetch=1,
            grid=(1,),
            in_specs=[anywhere] * (count + len(extra)),
            out_specs=anywhere,
            scratch_shapes=[
                pltpu.VMEM((2, 4, 512, 256), F32),
                pltpu.VMEM((2, 512, 4, 256), F32),
                pltpu.SemaphoreType.DMA((2, 4)),
                pltpu.SemaphoreType.DMA((2,)),
            ],
        ),
        out_shape=jax.ShapeDtypeStruct((4, 512, 4, 256), F32),
        input_output_aliases={1 + count: 0} if extra else {},
        compiler_params=pltpu.CompilerParams(vmem_limit_bytes=VMEM_LIMIT),
        cost_estimate=pl.CostEstimate(flops=0, bytes_accessed=8 << 20, transcendentals=0),
        name="fill_rows",
    )(where, *sources, *extra)


def upward(r, c, l):
    if l == 0:
        return r, (c & 4) | ((c + 1) & 3), l
    return (r & 4) | ((r + 1) & 3), c, l


def downward(r, c, l):
    if l == 0:
        return r, (c & 4) | ((c + 3) & 3), l
    return (r & 4) | ((r + 3) & 3), c, l


def first_hop(r, c, l):
    return (r, c ^ 4, l) if l == 0 else (c, r, l)


def first_hop_across(r, c, l):
    return (c, r, 1) if l == 0 else (r, c ^ 4, 0)


def second_hop(r, c, l):
    return (r ^ 4, c, l) if l == 1 else None


def row_up(r, c, l):
    return (r + 1) & 7, c, l


def row_down(r, c, l):
    return (r + 7) & 7, c, l


def column_straight(r, c, l):
    if (c, l) in ((0, 0), (7, 1)):
        return r, c, 1 - l
    return r, c + (1 if l else -1), l


def column_across(r, c, l):
    if (c, l) in ((0, 0), (7, 1)):
        return r, c, l
    return r, c + (1 if l else -1), 1 - l


def ring_straight(r, c, l):
    return r, (c & 4) | ((c + (1 if l else 3)) & 3), l


def ring_across(r, c, l):
    return r, (c & 4) | ((c + (1 if l else 3)) & 3), 1 - l


def ring_change(r, c, l):
    return (r, c ^ 4, l) if c in (0, 7) else None


def shards(matrix, transforms):
    barrier = lax.optimization_barrier
    row_pos = lax.axis_index("row")
    col_pos = lax.axis_index("col")
    layer_pos = lax.axis_index("layer")
    where = jnp.stack([row_pos, col_pos, layer_pos]).astype(jnp.int32)
    mine = transforms[0]

    lower = layer_pos == 0
    hop = send(mine, first_hop)
    hop_across = send(mine, first_hop_across)
    beside = in_chip(mine)
    hop, hop_across, beside, mine = barrier((hop, hop_across, beside, mine))
    block = jnp.stack([jnp.where(lower, mine, beside), jnp.where(lower, beside, mine)])
    hop = jnp.stack([jnp.where(lower, hop, hop_across), jnp.where(lower, hop_across, hop)])
    own = matrix.transpose(2, 0, 1, 3).reshape(4, 2048, 256)
    away = lax.dynamic_slice_in_dim(own, 2 * (1 - layer_pos), 2, 0)
    other = [in_chip(away[m]) for m in range(2)]
    start = jnp.where(lower, block, hop)
    up = send(start, upward)
    down = send(start, downward)
    far_side = send(hop, second_hop)
    start, up, down, far_side = barrier((start, up, down, far_side))
    partner = jnp.where(lower, hop, far_side)
    partner_up = send(partner, upward)
    partner_down = send(partner, downward)
    crossed = {i: in_chip(x) for i, x in zip(EARLY, (start, partner, up, down))}
    up, partner_up, partner_down, *early = barrier(
        (up, partner_up, partner_down, *[crossed[i] for i in EARLY])
    )
    crossed = dict(zip(EARLY, early))
    far = send(up, upward)
    partner_far = send(partner_down, downward)
    y = early_product(
        where,
        [start, partner, up, None, down],
        [crossed.get(i) for i in range(5)],
        own,
        other,
    )
    crossed[3], crossed[5] = in_chip(partner_up), in_chip(partner_down)
    far, partner_far, y, crossed[3], crossed[5] = barrier(
        (far, partner_far, y, crossed[3], crossed[5])
    )
    crossed[6], crossed[7] = in_chip(far), in_chip(partner_far)
    pieces = [start, partner, up, partner_up, down, partner_down, far, partner_far]
    crossed = [crossed[i] for i in range(8)]
    yh, yl, d_down, d_up, straight, across = moving_product(
        where, pieces, crossed, y, own, other
    )
    got_up = send(d_up, row_up)
    got_down = send(d_down, row_down)
    got_straight = send(straight, ring_straight)
    got_across = send(across, ring_across)
    across_beside = in_chip(across)
    w_down, w_up, still, beside = still_product(where, pieces, crossed, yh, yl)
    from_still = in_chip(beside)
    got_up, got_down, got_straight, got_across, across_beside, w_down, w_up, still = barrier(
        (got_up, got_down, got_straight, got_across, across_beside, w_down, w_up, still)
    )
    changed = send(jnp.where((col_pos == 0) == lower, got_across, got_straight), ring_change)
    edge_up = jnp.stack([w_up, from_still[3]])
    edge_down = jnp.stack([w_down, from_still[2]])
    still_got_up = send(edge_up, row_up)
    still_got_down = send(edge_down, row_down)

    top = jnp.where(row_pos == 0, d_down, got_up)
    bottom = jnp.where(row_pos == 7, d_up, got_down)
    inside = jnp.where(lower, col_pos > 0, col_pos < 7)
    then_straight = jnp.stack([jnp.where(inside, x[0], x[1]) for x in (top, bottom)])
    then_across = jnp.stack([jnp.where(inside, x[1], x[0]) for x in (top, bottom)])
    then_got_straight = send(then_straight, column_straight)
    then_got_across = send(then_across, column_across)
    def blocks(w, own, partner, kept, kept_beside, came_straight, came_across, came_changed):
        c, l = w[1], w[2]

        def both(condition, if_lower, if_upper):
            return [
                (condition & (l == which) & also, ref)
                for which, refs in ((0, if_lower), (1, if_upper))
                for also, ref in refs
            ]

        yes = c >= 0
        kept, kept_beside = [(yes, kept)], [(yes, kept_beside)]
        straight, across = [(yes, came_straight)], [(yes, came_across)]
        if came_changed is None:
            first, last = both(c > 0, across, straight), both(c < 7, straight, across)
        else:
            first = both((c > 0) & (c != 4), across, straight) + [(c == 4, came_changed)]
            last = both((c < 7) & (c != 3), straight, across) + [(c == 3, came_changed)]
        return [
            first + both(c == 0, own, partner),
            both(yes, partner, own),
            both(c > 0, own, partner) + both(c == 0, kept, kept_beside),
            last + both(c == 7, kept_beside, kept),
        ]

    def choose_stay(w, refs):
        still, beside, kept, kept_beside, came_straight, came_across, came_changed = refs
        yes = w[1] >= 0
        return [
            blocks(
                w,
                [(yes, still.at[k])],
                [(yes, beside.at[k])],
                kept.at[k],
                kept_beside.at[k],
                came_straight.at[k],
                came_across.at[k],
                came_changed.at[k],
            )
            for k in range(2)
        ]

    out = fill_rows(
        (1, 2),
        choose_stay,
        where,
        [still, from_still, straight, across_beside, got_straight, got_across, changed],
        None,
    )

    out, still_got_up, still_got_down = barrier((out, still_got_up, still_got_down))

    def choose_moved(w, refs):
        edge_up, edge_down, from_up, from_down, kept, came_straight, came_across = refs
        r = w[0]
        rows = [
            lambda n: [(r > 0, from_up.at[n]), (r == 0, edge_down.at[n])],
            lambda n: [(r < 7, from_down.at[n]), (r == 7, edge_up.at[n])],
        ]
        return [
            blocks(
                w,
                rows[k](0),
                rows[k](1),
                kept.at[k],
                came_straight.at[k],
                came_straight.at[k],
                came_across.at[k],
                None,
            )
            for k in range(2)
        ]

    return fill_rows(
        (0, 3),
        choose_moved,
        where,
        [
            edge_up,
            edge_down,
            still_got_up,
            still_got_down,
            then_across,
            then_got_straight,
            then_got_across,
        ],
        out,
    )


def solution(mesh):
    return jax.shard_map(
        shards,
        mesh=mesh,
        in_specs=(P("row", None, "col", "layer"), P(None, "row", ("col", "layer"), None)),
        out_specs=P("row", None, "col", "layer"),
        check_vma=False,
    )
```

```python
import jax
import jax.numpy as jnp
from jax import lax
from jax.experimental import pallas as pl
from jax.experimental.pallas import tpu as pltpu
from jax.sharding import PartitionSpec as P

F32 = jnp.float32
BF16 = jnp.bfloat16
AXES = ("row", "col", "layer")
VMEM_LIMIT = 58 * 1024 * 1024
EARLY = (0, 1, 2, 4)
LATE = (3, 5, 6, 7)
ANYWHERE = pl.BlockSpec(memory_space=pl.ANY)


def route(place):
    pairs = []
    for r in range(8):
        for c in range(8):
            for l in range(2):
                to = place(r, c, l)
                if to is not None:
                    pairs.append(((r * 8 + c) * 2 + l, (to[0] * 8 + to[1]) * 2 + to[2]))
    return pairs


def send(x, place):
    return lax.ppermute(x, AXES, route(place))


def in_chip(x):
    return lax.ppermute(x, "layer", [(0, 1), (1, 0)])


def split(x):
    high = x.astype(BF16)
    return high, (x - high.astype(F32)).astype(BF16)


def product(ah, al, bh, bl):
    def dot(a, b):
        return jnp.dot(a, b, preferred_element_type=F32)

    return dot(ah, bh) + (dot(ah, bl) + dot(al, bh))


def holders(i):
    up = (i & 4) | ((i + 3) & 3)
    down = (i & 4) | ((i + 1) & 3)
    far = (i & 4) | ((i + 2) & 3)
    return [i, i ^ 4, up, up ^ 4, down, down ^ 4, far, far ^ 4]


def turned(ref, index, pair, cols):
    rows = jnp.concatenate([ref[index, 0, pair, :, cols], ref[index, 1, pair, :, cols]], axis=0)
    return split(rows.T)


def halves_of_matrix(own_refs, other_refs, mh, ml):
    for n in range(4):
        for m in range(2):
            for k, block in enumerate((own_refs[n][m], other_refs[2 * n + m][...])):
                high, low = split(block)
                lanes = slice(m * 512 + k * 256, m * 512 + k * 256 + 256)
                mh[n * 128 : n * 128 + 128, lanes] = high
                ml[n * 128 : n * 128 + 128, lanes] = low


def early_kernel(where, *refs):
    ours, theirs = refs[:4], refs[4:8]
    own_refs, other_refs = refs[8:12], refs[12:20]
    y_ref, held, jh, jl, mh, ml, sem = refs[20:]
    pair = pl.program_id(0)
    layer = where[2]

    @pl.when(pair == 0)
    def _():
        for i in range(4):

            @pl.when(layer == 0)
            def _(i=i):
                pltpu.make_async_copy(ours[i], held.at[i], sem.at[i]).start()

            @pl.when(layer == 1)
            def _(i=i):
                pltpu.make_async_copy(theirs[i], held.at[i], sem.at[i]).start()

    halves_of_matrix(own_refs, other_refs, mh, ml)

    @pl.when(pair == 0)
    def _():
        for i in range(4):
            pltpu.make_async_copy(ours[i], held.at[i], sem.at[i]).wait()

    for i in range(4):
        for half in range(4):
            high, low = turned(held, i, pair, pl.ds(half * 256, 256))
            jh[half * 256 : half * 256 + 256, i * 128 : i * 128 + 128] = high
            jl[half * 256 : half * 256 + 256, i * 128 : i * 128 + 128] = low
    for a in range(4):
        rows = pl.ds(a * 256, 256)
        y_ref[rows, :] = product(jh[rows, :], jl[rows, :], mh[...], ml[...])


def matrix_pieces(which, pair_of):
    def rows(i):
        return lambda step, w: pair_of(step, w) * 8 + holders(w[1])[i]

    own = [pl.BlockSpec((2, 128, 256), lambda s, w, f=rows(i): (w[2], f(s, w), 0)) for i in which]
    other = [pl.BlockSpec((128, 256), lambda s, w, f=rows(i): (f(s, w), 0)) for i in which]
    return own + [spec for spec in other for m in range(2)]


def early_product(where, pieces, crossed, own, other):
    return pl.pallas_call(
        early_kernel,
        grid_spec=pltpu.PrefetchScalarGridSpec(
            num_scalar_prefetch=1,
            grid=(2,),
            in_specs=[ANYWHERE] * 8 + matrix_pieces(EARLY, lambda p, w: p),
            out_specs=pl.BlockSpec((1024, 1024), lambda p, w: (p, 0)),
            scratch_shapes=[
                pltpu.VMEM((4, 2, 2, 64, 1024), F32),
                pltpu.VMEM((1024, 512), BF16),
                pltpu.VMEM((1024, 512), BF16),
                pltpu.VMEM((512, 1024), BF16),
                pltpu.VMEM((512, 1024), BF16),
                pltpu.SemaphoreType.DMA((4,)),
            ],
        ),
        out_shape=jax.ShapeDtypeStruct((2048, 1024), F32),
        compiler_params=pltpu.CompilerParams(vmem_limit_bytes=VMEM_LIMIT),
        cost_estimate=pl.CostEstimate(
            flops=3 * 2 * 2048 * 512 * 1024, bytes_accessed=24 << 20, transcendentals=0
        ),
        name="early_product",
    )(
        where,
        *[pieces[i] for i in EARLY],
        *[crossed[i] for i in EARLY],
        *[own] * 4,
        *[other[m] for n in range(4) for m in range(2)],
    )


def by_role(slot, row_pos, down, up, stays):
    for s, condition, action in (
        (0, row_pos == 0, down),
        (0, row_pos > 0, lambda s: stays(s, 1)),
        (1, row_pos == 0, lambda s: stays(s, 1)),
        (1, row_pos > 0, down),
        (2, row_pos >= 0, up),
        (3, row_pos >= 0, lambda s: stays(s, 0)),
    ):

        @pl.when((slot == s) & condition)
        def _(s=s, action=action):
            action(s)


def fetch_columns(layer, ours, theirs, lane, held, sem):
    for core, sources in ((0, theirs), (1, ours)):

        @pl.when(layer == core)
        def _(core=core, sources=sources):
            for i in range(8):
                source = sources[i].at[:, core, :, pl.ds(lane(core) * 512, 512)]
                pltpu.make_async_copy(source, held.at[i], sem.at[i]).start()


def take_columns(row_pos, layer, held, sem, qh, ql):
    for i, start in enumerate(holders(row_pos)):
        pltpu.make_async_copy(held.at[i], held.at[i], sem.at[i]).wait()
        base = (start ^ (2 * layer)) * 128
        for half in range(2):
            high, low = split(held[i, half])
            rows = pl.ds(pl.multiple_of(base + half * 64, 64), 64)
            qh[rows, :] = high
            ql[rows, :] = low


def moving_kernel(where, *refs):
    ours, theirs = refs[:8], refs[8:16]
    y_ref = refs[16]
    own_refs, other_refs = refs[17:21], refs[21:29]
    yh, yl, d_down, d_up, straight, across = refs[29:35]
    held_a, held_b, jh, jl, mh, ml, qh, ql, done, sem_a, sem_b, sem_out = refs[35:]
    slot = pl.program_id(0)
    row_pos, layer = where[0], where[2]
    pair = slot // 2

    @pl.when(slot == 0)
    def _():
        for core, sources in ((0, ours), (1, theirs)):

            @pl.when(layer == core)
            def _(sources=sources):
                for n, i in enumerate(LATE):
                    pltpu.make_async_copy(sources[i], held_a.at[n], sem_a.at[n]).start()

        fetch_columns(layer, ours, theirs, lambda core: 1 - core, held_b, sem_b)

    @pl.when(slot % 2 == 0)
    def _():
        halves_of_matrix(own_refs, other_refs, mh, ml)

    @pl.when(slot == 0)
    def _():
        for n, i in enumerate(LATE):
            pltpu.make_async_copy(ours[i], held_a.at[n], sem_a.at[n]).wait()

    for n in range(4):
        for a in range(2):
            cols = pl.ds(pl.multiple_of((slot % 2) * 512 + a * 256, 256), 256)
            high, low = turned(held_a, n, pair, cols)
            jh[a * 256 : a * 256 + 256, n * 128 : n * 128 + 128] = high
            jl[a * 256 : a * 256 + 256, n * 128 : n * 128 + 128] = low

    for h in range(2):
        cols = slice(h * 512, h * 512 + 512)
        high, low = split(y_ref[:, cols] + product(jh[...], jl[...], mh[:, cols], ml[:, cols]))
        yh[:, cols] = high
        yl[:, cols] = low

    @pl.when(slot == 0)
    def _():
        take_columns(row_pos, layer, held_b, sem_b, qh, ql)

    for h in range(2):
        cols = slice(h * 256, h * 256 + 256)
        done[slot, h] = product(yh[...], yl[...], qh[:, cols], ql[:, cols])

    def leave(s, near, far):
        pltpu.make_async_copy(done.at[s, layer], near, sem_out.at[s, 0]).start()
        pltpu.make_async_copy(done.at[s, 1 - layer], far, sem_out.at[s, 1]).start()

    by_role(
        slot,
        row_pos,
        lambda s: leave(s, d_down.at[0], d_down.at[1]),
        lambda s: leave(s, d_up.at[0], d_up.at[1]),
        lambda s, k: leave(s, straight.at[k], across.at[k]),
    )

    @pl.when(slot == 3)
    def _():
        for s in range(4):
            for n in range(2):
                pltpu.make_async_copy(done.at[s, n], d_up.at[n], sem_out.at[s, n]).wait()


def still_kernel(where, *refs):
    ours, theirs = refs[:8], refs[8:16]
    yh, yl = refs[16:18]
    w_down, w_up, still, beside = refs[18:22]
    held_b, qh, ql, done, sem_b, sem_out = refs[22:]
    slot = pl.program_id(0)
    row_pos, layer = where[0], where[2]

    @pl.when(slot == 0)
    def _():
        fetch_columns(layer, ours, theirs, lambda core: core, held_b, sem_b)
        take_columns(row_pos, layer, held_b, sem_b, qh, ql)

    for h in range(2):
        cols = slice(h * 256, h * 256 + 256)
        done[slot, h] = product(yh[...], yl[...], qh[:, cols], ql[:, cols])

    def leave(s, near, far):
        pltpu.make_async_copy(done.at[s, layer], near, sem_out.at[s, 0]).start()
        pltpu.make_async_copy(done.at[s, 1 - layer], far, sem_out.at[s, 1]).start()

    by_role(
        slot,
        row_pos,
        lambda s: leave(s, w_down, beside.at[2]),
        lambda s: leave(s, w_up, beside.at[3]),
        lambda s, k: leave(s, still.at[k], beside.at[k]),
    )

    @pl.when(slot == 3)
    def _():
        for s in range(4):
            for n in range(2):
                pltpu.make_async_copy(done.at[s, n], w_up, sem_out.at[s, n]).wait()


ONE = jax.ShapeDtypeStruct((512, 256), F32)
TWO = jax.ShapeDtypeStruct((2, 512, 256), F32)
FOUR = jax.ShapeDtypeStruct((4, 512, 256), F32)
HALF = jax.ShapeDtypeStruct((2048, 1024), BF16)


def moving_product(where, pieces, crossed, y, own, other):
    block = pl.BlockSpec((512, 1024), lambda s, w: (s, 0))
    return pl.pallas_call(
        moving_kernel,
        grid_spec=pltpu.PrefetchScalarGridSpec(
            num_scalar_prefetch=1,
            grid=(4,),
            in_specs=[ANYWHERE] * 16 + [block] + matrix_pieces(LATE, lambda s, w: s // 2),
            out_specs=[block] * 2 + [ANYWHERE] * 4,
            scratch_shapes=[
                pltpu.VMEM((4, 2, 2, 64, 1024), F32),
                pltpu.VMEM((8, 2, 64, 512), F32),
                pltpu.VMEM((512, 512), BF16),
                pltpu.VMEM((512, 512), BF16),
                pltpu.VMEM((512, 1024), BF16),
                pltpu.VMEM((512, 1024), BF16),
                pltpu.VMEM((1024, 512), BF16),
                pltpu.VMEM((1024, 512), BF16),
                pltpu.VMEM((4, 2, 512, 256), F32),
                pltpu.SemaphoreType.DMA((4,)),
                pltpu.SemaphoreType.DMA((8,)),
                pltpu.SemaphoreType.DMA((4, 2)),
            ],
        ),
        out_shape=[HALF] * 2 + [TWO] * 4,
        compiler_params=pltpu.CompilerParams(vmem_limit_bytes=VMEM_LIMIT),
        cost_estimate=pl.CostEstimate(
            flops=3 * 2 * 2048 * 1024 * (512 + 512), bytes_accessed=36 << 20, transcendentals=0
        ),
        name="moving_product",
    )(where, *pieces, *crossed, y, *[own] * 4, *[other[m] for n in range(4) for m in range(2)])


def still_product(where, pieces, crossed, yh, yl):
    block = pl.BlockSpec((512, 1024), lambda s, w: (s, 0))
    return pl.pallas_call(
        still_kernel,
        grid_spec=pltpu.PrefetchScalarGridSpec(
            num_scalar_prefetch=1,
            grid=(4,),
            in_specs=[ANYWHERE] * 16 + [block] * 2,
            out_specs=[ANYWHERE] * 4,
            scratch_shapes=[
                pltpu.VMEM((8, 2, 64, 512), F32),
                pltpu.VMEM((1024, 512), BF16),
                pltpu.VMEM((1024, 512), BF16),
                pltpu.VMEM((4, 2, 512, 256), F32),
                pltpu.SemaphoreType.DMA((8,)),
                pltpu.SemaphoreType.DMA((4, 2)),
            ],
        ),
        out_shape=[ONE, ONE, TWO, FOUR],
        compiler_params=pltpu.CompilerParams(vmem_limit_bytes=VMEM_LIMIT),
        cost_estimate=pl.CostEstimate(
            flops=3 * 2 * 2048 * 1024 * 512, bytes_accessed=20 << 20, transcendentals=0
        ),
        name="still_product",
    )(where, *pieces, *crossed, yh, yl)


def fill_kernel(out_rows, choose, count, where, *refs):
    sources = refs[:count]
    out_ref, held, packed, in_sem, out_sem = refs[-5:]
    chosen = choose(where, sources)
    for k in range(2):
        for j in range(4):
            for condition, source in chosen[k][j]:

                @pl.when(condition)
                def _(source=source, k=k, j=j):
                    pltpu.make_async_copy(source, held.at[k, j], in_sem.at[k, j]).start()

    leaving = []
    for k in range(2):
        for j in range(4):
            pltpu.make_async_copy(chosen[k][j][0][1], held.at[k, j], in_sem.at[k, j]).wait()
            packed[k, :, j, :] = held[k, j]
        copy = pltpu.make_async_copy(packed.at[k], out_ref.at[out_rows[k]], out_sem.at[k])
        copy.start()
        leaving.append(copy)
    for copy in leaving:
        copy.wait()


def fill_rows(out_rows, choose, where, sources, previous):
    extra = [] if previous is None else [previous]
    count = len(sources)
    anywhere = pl.BlockSpec(memory_space=pl.ANY)

    def kernel(where, *refs):
        fill_kernel(out_rows, choose, count, where, *refs)

    return pl.pallas_call(
        kernel,
        grid_spec=pltpu.PrefetchScalarGridSpec(
            num_scalar_prefetch=1,
            grid=(1,),
            in_specs=[anywhere] * (count + len(extra)),
            out_specs=anywhere,
            scratch_shapes=[
                pltpu.VMEM((2, 4, 512, 256), F32),
                pltpu.VMEM((2, 512, 4, 256), F32),
                pltpu.SemaphoreType.DMA((2, 4)),
                pltpu.SemaphoreType.DMA((2,)),
            ],
        ),
        out_shape=jax.ShapeDtypeStruct((4, 512, 4, 256), F32),
        input_output_aliases={1 + count: 0} if extra else {},
        compiler_params=pltpu.CompilerParams(vmem_limit_bytes=VMEM_LIMIT),
        cost_estimate=pl.CostEstimate(flops=0, bytes_accessed=8 << 20, transcendentals=0),
        name="fill_rows",
    )(where, *sources, *extra)


def upward(r, c, l):
    if l == 0:
        return r, (c & 4) | ((c + 1) & 3), l
    return (r & 4) | ((r + 1) & 3), c, l


def downward(r, c, l):
    if l == 0:
        return r, (c & 4) | ((c + 3) & 3), l
    return (r & 4) | ((r + 3) & 3), c, l


def first_hop(r, c, l):
    return (r, c ^ 4, l) if l == 0 else (c, r, l)


def first_hop_across(r, c, l):
    return (c, r, 1) if l == 0 else (r, c ^ 4, 0)


def second_hop(r, c, l):
    return (r ^ 4, c, l) if l == 1 else None


def row_up(r, c, l):
    return (r + 1) & 7, c, l


def row_down(r, c, l):
    return (r + 7) & 7, c, l


def still_up(r, c, l):
    return (r + 1, c, l) if r < 7 else None


def still_down(r, c, l):
    return (r - 1, c, l) if r > 0 else None


def column_straight(r, c, l):
    if (c, l) in ((0, 0), (7, 1)):
        return r, c, 1 - l
    return r, c + (1 if l else -1), l


def column_across(r, c, l):
    if (c, l) in ((0, 0), (7, 1)):
        return r, c, l
    return r, c + (1 if l else -1), 1 - l


def ring_straight(r, c, l):
    return r, (c & 4) | ((c + (1 if l else 3)) & 3), l


def ring_across(r, c, l):
    return r, (c & 4) | ((c + (1 if l else 3)) & 3), 1 - l


def ring_change(r, c, l):
    return (r, c ^ 4, l) if c in (0, 7) else None


def shards(matrix, transforms):
    barrier = lax.optimization_barrier
    row_pos = lax.axis_index("row")
    col_pos = lax.axis_index("col")
    layer_pos = lax.axis_index("layer")
    where = jnp.stack([row_pos, col_pos, layer_pos]).astype(jnp.int32)
    mine = transforms[0]

    lower = layer_pos == 0
    hop = send(mine, first_hop)
    hop_across = send(mine, first_hop_across)
    beside = in_chip(mine)
    hop, hop_across, beside, mine = barrier((hop, hop_across, beside, mine))
    block = jnp.stack([jnp.where(lower, mine, beside), jnp.where(lower, beside, mine)])
    hop = jnp.stack([jnp.where(lower, hop, hop_across), jnp.where(lower, hop_across, hop)])
    own = matrix.transpose(2, 0, 1, 3).reshape(4, 2048, 256)
    away = lax.dynamic_slice_in_dim(own, 2 * (1 - layer_pos), 2, 0)
    other = [in_chip(away[m]) for m in range(2)]
    start = jnp.where(lower, block, hop)
    up = send(start, upward)
    down = send(start, downward)
    far_side = send(hop, second_hop)
    start, up, down, far_side = barrier((start, up, down, far_side))
    partner = jnp.where(lower, hop, far_side)
    partner_up = send(partner, upward)
    partner_down = send(partner, downward)
    crossed = {i: in_chip(x) for i, x in zip(EARLY, (start, partner, up, down))}
    up, partner_up, partner_down, *early = barrier(
        (up, partner_up, partner_down, *[crossed[i] for i in EARLY])
    )
    crossed = dict(zip(EARLY, early))
    far = send(up, upward)
    partner_far = send(partner_down, downward)
    y = early_product(
        where,
        [start, partner, up, None, down],
        [crossed.get(i) for i in range(5)],
        own,
        other,
    )
    crossed[3], crossed[5] = in_chip(partner_up), in_chip(partner_down)
    far, partner_far, y, crossed[3], crossed[5] = barrier(
        (far, partner_far, y, crossed[3], crossed[5])
    )
    crossed[6], crossed[7] = in_chip(far), in_chip(partner_far)
    pieces = [start, partner, up, partner_up, down, partner_down, far, partner_far]
    crossed = [crossed[i] for i in range(8)]
    yh, yl, d_down, d_up, straight, across = moving_product(
        where, pieces, crossed, y, own, other
    )
    got_up = send(d_up, row_up)
    got_down = send(d_down, row_down)
    got_straight = send(straight, ring_straight)
    got_across = send(across, ring_across)
    across_beside = in_chip(across)
    w_down, w_up, still, beside = still_product(where, pieces, crossed, yh, yl)
    got_up, got_down, got_straight, got_across, across_beside, w_down, w_up, still, beside = barrier(
        (got_up, got_down, got_straight, got_across, across_beside, w_down, w_up, still, beside)
    )
    changed = send(jnp.where((col_pos == 0) == lower, got_across, got_straight), ring_change)
    from_still = in_chip(beside)
    edge_up = jnp.stack([w_up, from_still[3]])
    edge_down = jnp.stack([w_down, from_still[2]])
    still_got_up = send(edge_up, still_up)
    still_got_down = send(edge_down, still_down)

    top = jnp.where(row_pos == 0, d_down, got_up)
    bottom = jnp.where(row_pos == 7, d_up, got_down)
    inside = jnp.where(lower, col_pos > 0, col_pos < 7)
    then_straight = jnp.stack([jnp.where(inside, x[0], x[1]) for x in (top, bottom)])
    then_across = jnp.stack([jnp.where(inside, x[1], x[0]) for x in (top, bottom)])
    then_got_straight = send(then_straight, column_straight)
    then_got_across = send(then_across, column_across)
    def blocks(w, own, partner, kept, kept_beside, came_straight, came_across, came_changed):
        c, l = w[1], w[2]

        def both(condition, if_lower, if_upper):
            return [
                (condition & (l == which) & also, ref)
                for which, refs in ((0, if_lower), (1, if_upper))
                for also, ref in refs
            ]

        yes = c >= 0
        kept, kept_beside = [(yes, kept)], [(yes, kept_beside)]
        straight, across = [(yes, came_straight)], [(yes, came_across)]
        if came_changed is None:
            first, last = both(c > 0, across, straight), both(c < 7, straight, across)
        else:
            first = both((c > 0) & (c != 4), across, straight) + [(c == 4, came_changed)]
            last = both((c < 7) & (c != 3), straight, across) + [(c == 3, came_changed)]
        return [
            first + both(c == 0, own, partner),
            both(yes, partner, own),
            both(c > 0, own, partner) + both(c == 0, kept, kept_beside),
            last + both(c == 7, kept_beside, kept),
        ]

    def choose_stay(w, refs):
        still, beside, kept, kept_beside, came_straight, came_across, came_changed = refs
        yes = w[1] >= 0
        return [
            blocks(
                w,
                [(yes, still.at[k])],
                [(yes, beside.at[k])],
                kept.at[k],
                kept_beside.at[k],
                came_straight.at[k],
                came_across.at[k],
                came_changed.at[k],
            )
            for k in range(2)
        ]

    out = fill_rows(
        (1, 2),
        choose_stay,
        where,
        [still, from_still, straight, across_beside, got_straight, got_across, changed],
        None,
    )

    def choose_moved(w, refs):
        edge_up, edge_down, from_up, from_down, kept, came_straight, came_across = refs
        r = w[0]
        rows = [
            lambda n: [(r > 0, from_up.at[n]), (r == 0, edge_down.at[n])],
            lambda n: [(r < 7, from_down.at[n]), (r == 7, edge_up.at[n])],
        ]
        return [
            blocks(
                w,
                rows[k](0),
                rows[k](1),
                kept.at[k],
                came_straight.at[k],
                came_straight.at[k],
                came_across.at[k],
                None,
            )
            for k in range(2)
        ]

    return fill_rows(
        (0, 3),
        choose_moved,
        where,
        [
            edge_up,
            edge_down,
            still_got_up,
            still_got_down,
            then_across,
            then_got_straight,
            then_got_across,
        ],
        out,
    )


def solution(mesh):
    return jax.shard_map(
        shards,
        mesh=mesh,
        in_specs=(P("row", None, "col", "layer"), P(None, "row", ("col", "layer"), None)),
        out_specs=P("row", None, "col", "layer"),
        check_vma=False,
    )
```
